128 devices in a mesh: offset: 4 (over x), mid: 8 (over z, core), tm: 4 (over y).
Axes of the slice: x: 4, y: 4, z: 4, core: 2. Of those that a mesh axis runs over, the one named last changes fastest.
Arguments:
- traces: bfloat16 [32768, 1024], P(('offset', 'mid'), 'tm'), may hold values from -6 to 6
- dest: int32 [32768, 1], P(('offset', 'mid')), may hold values from 0 to 31; in each aligned block of 1024 rows (0 to 1023, 1024 to 2047, ...) at most 64 rows name the same one
- cell: int32 [32768, 1], P(('offset', 'mid')), may hold values from 0 to 511
- w_first: bfloat16 [16, 9], replicated, may hold values from -2 to 2
- w_mid: bfloat16 [2, 16, 144], replicated, may hold values from -0.5 to 0.5
- w_last: bfloat16 [1, 144], replicated, may hold values from -0.5 to 0.5
- bias: float32 [3, 16], replicated, may hold values from -3 to 3
Outputs:
- denoised: float32 [32, 512, 1024], P('offset', 'mid', 'tm')
The draws below stay inside these ranges and needn't reach their ends.
Inputs may be any that keep to these rules, and one draw needn't show every extreme that they name: `dest`: among the traces of one device no owner is named more than 64 times, a bound that some block reaches.
All inputs are finite; a program needn't handle non-finite values.
Results may differ from the reference program's by a relative error of at most 0.0038.
Values may be sent and summed in bfloat16 or wider, within the bound.
No kernel may reach another device: no remote copies, remote signals or barrier semaphores. Data moves between devices by JAX's collectives and lax.ppermute only.
A program may use at most 256 MiB of HBM per device.

```python
import math
import jax
import jax.numpy as jnp
import numpy as np
from jax import lax

CH = 16
TR_DEV = 1024
MID_DEV = 64
NDEST = 32
CAP = 64
CL_DEV = 8
TRACES = 32768
NT = 1024
N_OFFSET = 4
N_MID = 8


def plant(entries, rng, least, high):
    longest = entries.shape.index(max(entries.shape))
    spots = []
    for shift in (0, 1):
        where = [jax.random.randint(jax.random.fold_in(rng, axis), (), 0, length) for axis, length in enumerate(entries.shape)]
        where[longest] = (where[longest] + shift) % entries.shape[longest]
        spots.append(tuple(where))
    return entries.at[spots[0]].set(least).at[spots[1]].set(high)


def level_of(rng, dims, pieces, least, high):
    level = 1.0
    for dim, blocks in pieces:
        steps = jax.random.uniform(jax.random.fold_in(jax.random.fold_in(rng, 6), dim), (blocks,), jnp.float32, least / len(pieces), high / len(pieces))
        level = level * jnp.repeat(jnp.exp(steps), dims[dim] // blocks).reshape((-1,) + (1,) * (len(dims) - 1 - dim))
    return level


def shared_out(own_key, own, number, rows, count, top, reach, skew):
    ranking = jax.random.permutation(own_key, count)
    packed, usual = load_shares(count, rows * top, reach, skew, True), load_shares(count, rows * top, reach, skew, False)
    places = jnp.arange(count)

    def named(tallies, rotation):
        used = int((tallies > 0).sum())
        fixed = max(1, used // 4)
        shifted = fixed + (places - fixed + rotation * (used - fixed)) % max(1, count - fixed)
        return jnp.zeros((count,), jnp.int32).at[ranking[jnp.where(places < fixed, places, shifted)]].set(jnp.asarray(tallies, jnp.int32))

    tallies = jnp.where(number % 4 == 0, named(packed, number // 4), named(usual, number - number // 4 - 1))
    mixed = jax.random.permutation(jax.random.fold_in(own, 3), count)
    donor, sink = mixed[0:count // 2 * 2:2], mixed[1:count // 2 * 2:2]
    slack = jnp.minimum(tallies[donor] - 1, reach - tallies[sink]) // 2
    slack = jnp.where((donor == ranking[0]) | (sink == ranking[0]) | (tallies[sink] == 0), 0, jnp.maximum(slack, 0))
    shifted = jax.random.randint(jax.random.fold_in(own, 4), (count // 2,), 0, 1 << 20) % (slack + 1)
    tallies = tallies.at[donor].add(-shifted).at[sink].add(shifted)
    labels = jnp.searchsorted(jnp.cumsum(tallies), jnp.arange(rows * top), side="right").astype(jnp.int32)
    listing = labels.reshape(top, rows).T
    listing = listing[jax.random.permutation(jax.random.fold_in(own, 1), rows)]
    rotation = jax.random.randint(jax.random.fold_in(own, 2), (rows, 1), 0, top)
    return jnp.take_along_axis(listing, (jnp.arange(top)[None, :] + rotation) % top, axis=1)


def load_shares(number_of, total, limit, slope, full):
    loads = [(1 << 20) // math.isqrt(standing ** slope) + 1 for standing in range(1, number_of + 1)]
    largest = limit if full else min(limit, max(-(-total // number_of), total * loads[0] // sum(loads)))
    least = 1 if total - largest >= number_of - 1 else 0
    holding, rest = [largest] + [least] * (number_of - 1), total - largest - least * (number_of - 1)
    while rest > 0:
        movable = [i for i in range(1, number_of) if holding[i] < largest] or [i for i in range(1, number_of) if holding[i] < limit]
        whole, left = sum([loads[i] for i in movable]), rest
        for i in movable:
            addition = min(limit - holding[i], max(1, left * loads[i] // whole), rest)
            holding[i] = holding[i] + addition
            rest = rest - addition
    return np.array(holding)


def bell_draw(own_key, extent, spread, most, split=(), held_as=jnp.bfloat16):
    entries = spread * jax.random.normal(own_key, extent, jnp.float32)
    if split:
        entries = entries * level_of(own_key, extent, split, -0.22, 0.18)
    return jnp.clip(entries, -most, most).astype(held_as)


def setup_inputs(seed: int = 0) -> dict:
    seeds = jax.random.split(jax.random.key(seed), 8)
    traces = bell_draw(seeds[0], (TRACES, NT), 1.0, 6.0, ((0, 32), (1, 4)))
    dest_keys = jax.random.split(jax.random.fold_in(seeds[1], 1), TRACES // TR_DEV)
    dest_turns = jax.random.permutation(jax.random.fold_in(seeds[1], 3), TRACES // TR_DEV)
    dest = jax.vmap(lambda own, number: shared_out(jax.random.fold_in(seeds[1], 2), own, number, TR_DEV, NDEST, 1, CAP, 2))(dest_keys, dest_turns).reshape((TRACES, 1))
    cell = plant(jax.random.randint(seeds[2], (TRACES, 1), 0, CL_DEV * MID_DEV), jax.random.fold_in(seeds[2], 1), 0, (CL_DEV * MID_DEV) - 1).astype(jnp.int32)
    w_first = bell_draw(seeds[3], (CH, 9), 9 ** -0.5, 2.0)
    w_mid = bell_draw(seeds[4], (2, CH, 9 * CH), (9 * CH) ** -0.5, 0.5)
    w_last = bell_draw(seeds[5], (1, 9 * CH), (9 * CH) ** -0.5, 0.5)
    bias = bell_draw(seeds[6], (3, CH), 0.5, 3.0, (), jnp.float32)
    return {"traces": traces, "dest": dest, "cell": cell, "w_first": w_first, "w_mid": w_mid, "w_last": w_last, "bias": bias}


DILATIONS = (1, 2, 4, 1)


def convolve(image, weight, dilation):
    rows = image.shape[1]
    cols = image.shape[2]
    padded = jnp.pad(image, ((0, 0), (dilation, dilation), (dilation, dilation)))
    taps = jnp.concatenate([padded[:, a * dilation:a * dilation + rows, b * dilation:b * dilation + cols] for a in range(3) for b in range(3)], 0)
    return jnp.einsum("ok,kmt->omt", weight.astype(jnp.float32), taps.astype(jnp.float32))


def network(image, w_first, w_mid, w_last, bias):
    weights = (w_first, w_mid[0], w_mid[1], w_last)
    active = image[None]
    output = None
    for layer in range(4):
        output = convolve(active, weights[layer], DILATIONS[layer])
        if layer < 3:
            active = jax.nn.gelu(output + bias[layer][:, None, None]).astype(jnp.bfloat16)
    return output[0]


def reference(traces, dest, cell, w_first, w_mid, w_last, bias):
    target = dest[:, 0]
    local = cell[:, 0]
    ncls = CL_DEV * N_OFFSET
    nmid = MID_DEV * N_MID
    klass = (target // N_MID) * CL_DEV + local // MID_DEV
    midpoint = (target % N_MID) * MID_DEV + local % MID_DEV
    flat = (klass * nmid + midpoint).astype(jnp.int32)
    sums = jax.ops.segment_sum(traces.astype(jnp.float32), flat, num_segments=ncls * nmid)
    fold = jax.ops.segment_sum(jnp.ones(flat.shape, jnp.float32), flat, num_segments=ncls * nmid)
    stack = (sums / jnp.maximum(fold, 1.0)[:, None]).astype(jnp.bfloat16).reshape(ncls, nmid, -1)
    noise = lax.map(lambda image: network(image, w_first, w_mid, w_last, bias), stack)
    return stack.astype(jnp.float32) - noise
```

```python
import functools

import jax
import jax.numpy as jnp
from jax import lax
from jax.experimental import pallas as pl
from jax.experimental.pallas import tpu as pltpu
from jax.sharding import PartitionSpec as P

BF = jnp.bfloat16
F32 = jnp.float32
OWNERS = 32
SLOTS = 64
COUNT = 1024
TS = 256
CL = 8
MB = 64
HALO = 8
SEG = TS + 2 * HALO
LANES = CL * SEG
CHUNK = 256
NCHUNK = 9
WIDE = CHUNK * NCHUNK
PAD = 128
CH = 16
R1, R2, R3 = 78, 74, 66
N2, N3 = 13, 12
EXTRA = 8
PAY = SLOTS + EXTRA


def slots_of(rows, groups):
    return [r for g in range(groups) for r in range(g, rows, groups)]


ORDER1 = slots_of(R1, 2)
ORDER2 = slots_of(R2, 4)
SLOT2 = {r: s for s, r in enumerate(ORDER2)}


def iota(shape, dim):
    return lax.broadcasted_iota(jnp.int32, shape, dim)


def onehot(mask):
    return jnp.where(mask, 1.0, 0.0).astype(BF)


def dot(a, b):
    return jnp.dot(a, b, preferred_element_type=F32)


def dot_t(a, b):
    return lax.dot_general(a, b, (((1,), (1,)), ((), ())), preferred_element_type=F32)


def edges_kernel(traces_ref, left_ref, right_ref):
    row = iota((2 * HALO, TS), 0)
    col = iota((2 * HALO, TS), 1)
    pick = onehot(col == jnp.where(row < HALO, row, TS - 2 * HALO + row))
    out = dot_t(pick, traces_ref[...])
    left_ref[...] = out[:HALO].astype(BF)
    right_ref[...] = out[HALO:].astype(BF)


def send_kernel(dest_ref, cell_ref, low_ref, high_ref, traces_ref, out_ref, token_ref):
    dest = dest_ref[...]
    cell = cell_ref[...]
    hot = iota((OWNERS, COUNT), 0) == dest
    upper = onehot(iota((COUNT, COUNT), 0) < iota((COUNT, COUNT), 1))
    before = dot(onehot(hot), upper)
    rank = jnp.sum(jnp.where(hot, before, 0.0), axis=0, keepdims=True)
    place = dest * SLOTS + rank.astype(jnp.int32)
    high = (cell >> 5) + 1
    low = cell & 31
    meta = jnp.concatenate([high, low, jnp.zeros((EXTRA - 2, COUNT), jnp.int32)], axis=0)
    meta = jnp.concatenate(
        [low_ref[...].astype(F32), high_ref[...].astype(F32), meta.astype(F32), jnp.zeros((EXTRA, COUNT), F32)], axis=0
    ).astype(BF)
    traces = traces_ref[...]
    step = 4
    for o in range(0, OWNERS, step):
        slot = iota((step * SLOTS, COUNT), 0) + o * SLOTS
        placing = onehot(slot == place)
        rows = dot(placing, traces).astype(BF)
        extra = dot_t(meta, placing)
        for k in range(step):
            out_ref[o + k, 0:SLOTS, :] = rows[k * SLOTS : (k + 1) * SLOTS]
            part = extra[:, k * SLOTS : (k + 1) * SLOTS]
            out_ref[o + k, SLOTS:PAY, :] = jnp.concatenate(
                [part[EXTRA * q : EXTRA * (q + 1)] for q in range(4)], axis=1
            ).astype(BF)
    token_ref[...] = jnp.zeros(token_ref.shape, F32) + rank[:, 0:128]


def weights_kernel(first_ref, mid_ref, last_ref, token_ref, w1_ref, w2_ref, w3_ref, w4_ref):
    rows = R1 * CH
    first = first_ref[...]
    spread = onehot((iota((rows, CH), 0) & (CH - 1)) == iota((rows, CH), 1))
    base = dot(spread, first).astype(BF)
    r = iota((rows, 240), 0) >> 4
    r = jnp.where(r < R1 // 2, 2 * r, 2 * r - (R1 - 1))
    c = iota((rows, 240), 1)
    b = jnp.where(c >= 80, 1, 0) + jnp.where(c >= 160, 1, 0)
    delta = c - 80 * b - r
    ck = iota((9, 240), 1)
    bk = jnp.where(ck >= 80, 1, 0) + jnp.where(ck >= 160, 1, 0)
    total = jnp.zeros((rows, 240), F32)
    for a in range(3):
        pick = onehot(iota((9, 240), 0) == 3 * a + bk)
        total = jnp.where(delta == a, dot(base, pick), total)
    w1_ref[...] = (0.5 * total).astype(BF)
    for layer, out_ref, width in ((0, w2_ref, N2), (1, w3_ref, N3)):
        rows = width * CH
        spread = onehot((iota((rows, CH), 0) & (CH - 1)) == iota((rows, CH), 1))
        base = dot(spread, mid_ref[layer]).astype(BF)
        delta = ((iota((rows, 768), 1) >> 4) & 15) - (iota((rows, 768), 0) >> 4)
        col = iota((144, 768), 1)
        total = jnp.zeros((rows, 768), F32)
        for a in range(3):
            pick = onehot(iota((144, 768), 0) == (3 * a + (col >> 8)) * CH + (col & 15))
            total = jnp.where(delta == a, dot(base, pick), total)
        out_ref[...] = (0.5 * total).astype(BF)
    cols = R3 * CH
    delta = (iota((MB, cols), 1) >> 4) - iota((MB, cols), 0)
    col = iota((144, cols), 1) & 15
    last = last_ref[...]
    for b in range(3):
        total = jnp.zeros((MB, cols), F32)
        for a in range(3):
            pick = onehot(iota((144, cols), 0) == (3 * a + b) * CH + col)
            line = dot(jnp.broadcast_to(last, (8, 144)), pick)[0:1]
            total = jnp.where(delta == a, line, total)
        w4_ref[b * MB : (b + 1) * MB, :] = total.astype(BF)


def stack_kernel(recv_ref, out_ref, low_ref, high_ref):
    cells, sides = [], [[], []]
    for s in range(OWNERS):
        extra = recv_ref[s, SLOTS:PAY, :].astype(F32)
        sides[0].append(extra[:, 0:SLOTS])
        sides[1].append(extra[:, SLOTS : 2 * SLOTS])
        cells.append((extra[0:1, 128:192] - 1.0) * 32.0 + extra[1:2, 128:192])
    cell = jnp.concatenate(cells, axis=1).astype(jnp.int32)
    total = OWNERS * SLOTS
    side = jnp.concatenate(
        [jnp.concatenate(sides[0], axis=1), jnp.concatenate(sides[1], axis=1), jnp.ones((16, total), F32)], axis=0
    ).astype(BF)
    rows = recv_ref[:, 0:SLOTS, :].reshape(total, TS)
    for c in range(CL):
        select = onehot(iota((MB, total), 0) + c * MB == cell)
        sums = dot(select, rows)
        more = dot_t(select, side)
        fold = jnp.maximum(more[:, 16:17], 1.0)
        full = jnp.concatenate([more[:, 0:HALO], sums, more[:, HALO : 2 * HALO]], axis=1)
        part = (full / fold).astype(BF)
        out_ref[:, c * SEG : (c + 1) * SEG] = part
    low_ref[...] = out_ref[0:HALO, :]
    high_ref[...] = out_ref[MB - HALO : MB, :]


def gelu_half(h):
    c0 = 2.0 * 0.7978845608028654
    c1 = 8.0 * 0.7978845608028654 * 0.044715
    return h + h * jnp.tanh(h * (c0 + c1 * (h * h)))


def conv_kernel(pos_ref, stack_ref, low_ref, high_ref, w1_ref, w2_ref, w3_ref, w4_ref, bias_ref, out_ref,
                x_ref, h1_ref, h2_ref, h3_ref, p_ref, mask_ref):
    mid = pos_ref[0]
    tm = pos_ref[1]
    lane = iota((CH, WIDE), 1)
    tau = lane
    for c in range(1, CL):
        tau = tau - jnp.where(lane >= c * SEG, SEG, 0)
    t = tau - HALO + tm * TS
    keep = jnp.where((t >= 0) & (t < 4 * TS) & (lane < LANES), 1.0, 0.0)
    mask_ref[0] = keep.astype(BF)
    mask_ref[1] = (keep * jnp.where(mid > 0, 1.0, 0.0)).astype(BF)
    mask_ref[2] = (keep * jnp.where(mid < 7, 1.0, 0.0)).astype(BF)
    x_ref[...] = jnp.zeros(x_ref.shape, BF)
    image = jnp.concatenate([low_ref[...].astype(F32), stack_ref[...].astype(F32), high_ref[...].astype(F32)], axis=0).astype(BF)
    x_ref[0:80, 1:LANES] = image[:, : LANES - 1]
    x_ref[80:160, 0:LANES] = image
    x_ref[160:240, 0 : LANES - 1] = image[:, 1:]
    zeros = jnp.zeros((h1_ref.shape[0], PAD), BF)
    h1_ref[:, 0:PAD] = zeros
    h1_ref[:, PAD + WIDE :] = zeros
    h1_ref[R1 * CH :, :] = jnp.zeros((h1_ref.shape[0] - R1 * CH, h1_ref.shape[1]), BF)
    zeros = jnp.zeros((h2_ref.shape[0], PAD), BF)
    h2_ref[:, 0:PAD] = zeros
    h2_ref[:, PAD + WIDE :] = zeros
    h2_ref[R2 * CH :, :] = jnp.zeros((h2_ref.shape[0] - R2 * CH, h2_ref.shape[1]), BF)
    biases = [jnp.broadcast_to(0.5 * bias_ref[k], (CH, CHUNK)) for k in range(3)]

    def finish(acc, k, row, base, into_ref, at, lead):
        g = gelu_half(acc + biases[k])
        which = 1 if row < 0 else (2 if row >= MB else 0)
        g = g.astype(BF) * mask_ref[which, :, pl.ds(base, CHUNK)]
        into_ref[at * CH : (at + 1) * CH, pl.ds(base + lead, CHUNK)] = g

    def layer1(n, _):
        base = pl.multiple_of(n * CHUNK, CHUNK)
        x = x_ref[:, pl.ds(base, CHUNK)]
        for s0 in range(0, R1, 13):
            acc = dot(w1_ref[s0 * CH : (s0 + 13) * CH, :], x)
            for j in range(13):
                finish(acc[j * CH : (j + 1) * CH], 0, ORDER1[s0 + j] - 7, base, h1_ref, s0 + j, PAD)
        return 0

    lax.fori_loop(0, NCHUNK, layer1, 0)

    def window(ref, s0, base, d):
        wide = ref[s0 * CH : s0 * CH + 256, pl.ds(base, CHUNK + 2 * PAD)]
        return jnp.concatenate(
            [wide[:, PAD - d : PAD - d + CHUNK], wide[:, PAD : PAD + CHUNK], wide[:, PAD + d : PAD + d + CHUNK]], axis=0
        )

    def layer2(n, _):
        base = pl.multiple_of(n * CHUNK, CHUNK)
        for s0 in range(0, R1 - 2, N2):
            acc = dot(w2_ref[...], window(h1_ref, s0, base, 2))
            for j in range(N2):
                if s0 + j < R1 and ORDER1[s0 + j] < R2:
                    q = ORDER1[s0 + j]
                    finish(acc[j * CH : (j + 1) * CH], 1, q - 5, base, h2_ref, SLOT2[q], PAD)
        return 0

    lax.fori_loop(0, NCHUNK, layer2, 0)

    def layer3(n, _):
        base = pl.multiple_of(n * CHUNK, CHUNK)
        for s0 in range(0, R2 - 2, N3):
            acc = dot(w3_ref[...], window(h2_ref, s0, base, 4))
            for j in range(N3):
                if s0 + j < R2 and ORDER2[s0 + j] < R3:
                    q = ORDER2[s0 + j]
                    finish(acc[j * CH : (j + 1) * CH], 2, q - 1, base, h3_ref, q, 0)
        return 0

    lax.fori_loop(0, NCHUNK, layer3, 0)

    def layer4(n, _):
        base = pl.multiple_of(n * CHUNK, CHUNK)
        p_ref[:, pl.ds(base, CHUNK)] = dot(w4_ref[...], h3_ref[:, pl.ds(base, CHUNK)])
        return 0

    lax.fori_loop(0, NCHUNK, layer4, 0)
    for c in range(CL):
        at = c * SEG + HALO
        noise = (
            p_ref[0:MB, at - 1 : at - 1 + TS] + p_ref[MB : 2 * MB, at : at + TS] + p_ref[2 * MB :, at + 1 : at + 1 + TS]
        )
        out_ref[c] = stack_ref[:, at : at + TS].astype(F32) - noise


def call(kernel, outs, scratch=(), smem=0, n=0, name=None):
    specs = [pl.BlockSpec(memory_space=pltpu.SMEM) for _ in range(smem)]
    specs += [pl.BlockSpec(memory_space=pltpu.VMEM) for _ in range(n)]
    return pl.pallas_call(
        kernel,
        out_shape=outs,
        in_specs=specs,
        out_specs=jax.tree.map(lambda _: pl.BlockSpec(memory_space=pltpu.VMEM), outs),
        scratch_shapes=list(scratch),
        compiler_params=pltpu.CompilerParams(vmem_limit_bytes=60000 * 1024),
        name=name,
    )


def shape(*dims, dtype=BF):
    return jax.ShapeDtypeStruct(dims, dtype)


def edges(traces):
    return call(edges_kernel, (shape(HALO, COUNT), shape(HALO, COUNT)), n=1, name="edges")(traces)


def build_send(dest, cell, low, high, traces):
    return call(send_kernel, (shape(OWNERS, PAY, TS), shape(8, 128, dtype=F32)), n=5, name="send")(
        dest, cell, low, high, traces
    )


def build_weights(w_first, w_mid, w_last, token):
    outs = (shape(R1 * CH, 240), shape(N2 * CH, 768), shape(N3 * CH, 768), shape(3 * MB, R3 * CH))
    return call(weights_kernel, outs, n=4, name="weights")(w_first, w_mid, w_last, token)


def build_stack(recv):
    outs = (shape(MB, LANES), shape(HALO, LANES), shape(HALO, LANES))
    return call(stack_kernel, outs, n=1, name="stack")(recv)


def convolve(pos, stack, low, high, weights, bias):
    scratch = [
        pltpu.VMEM((240, WIDE), BF),
        pltpu.VMEM((81 * CH, WIDE + 2 * PAD), BF),
        pltpu.VMEM((76 * CH, WIDE + 2 * PAD), BF),
        pltpu.VMEM((R3 * CH, WIDE), BF),
        pltpu.VMEM((3 * MB, WIDE), F32),
        pltpu.VMEM((3, CH, WIDE), BF),
    ]
    return call(conv_kernel, shape(CL, MB, TS, dtype=F32), scratch, smem=1, n=8, name="conv")(
        pos, stack, low, high, *weights, bias
    )


def neighbours(low_edge, high_edge, axis):
    count = lax.axis_size(axis)
    up = [(i, i + 1) for i in range(count - 1)]
    down = [(b, a) for a, b in up]
    return lax.ppermute(high_edge, axis, up), lax.ppermute(low_edge, axis, down)


def shards(traces, dest, cell, w_first, w_mid, w_last, bias):
    left, right = edges(traces)
    low, high = neighbours(left, right, "tm")
    send, token = build_send(dest.reshape(1, COUNT), cell.reshape(1, COUNT), low, high, traces)
    recv = lax.all_to_all(send, ("offset", "mid"), split_axis=0, concat_axis=0, tiled=True)
    weights = build_weights(w_first, w_mid, w_last, token)
    stack, low_rows, high_rows = build_stack(recv)
    below, above = neighbours(low_rows, high_rows, "mid")
    pos = jnp.stack([lax.axis_index("mid"), lax.axis_index("tm")]).astype(jnp.int32)
    return convolve(pos, stack, below, above, weights, bias.reshape(3, CH, 1))


def solution(mesh):
    rows = P(("offset", "mid"), "tm")
    column = P(("offset", "mid"), None)
    placed = (rows, column, column, P(), P(), P(), P())
    return jax.shard_map(
        shards, mesh=mesh, in_specs=placed, out_specs=P("offset", "mid", "tm"), check_vma=False
    )
```

```python
import functools

import jax
import jax.numpy as jnp
from jax import lax
from jax.experimental import pallas as pl
from jax.experimental.pallas import tpu as pltpu
from jax.sharding import PartitionSpec as P

BF = jnp.bfloat16
F32 = jnp.float32
OWNERS = 32
SLOTS = 64
COUNT = 1024
TS = 256
CL = 8
MB = 64
HALO = 8
SEG = TS + 2 * HALO
LANES = CL * SEG
TILE = 128
TILES = 17
CHUNK = 2 * TILE
NCHUNK = 9
WIDE = CHUNK * NCHUNK
LEAD = 4
EXT = (LEAD + 22) * TILE
CH = 16
R1, R2, R3 = 78, 74, 66
TAPS = 240
KDIM = 256
GROUP = 3
EXTRA = 8
PAY = SLOTS + EXTRA


def slots_of(rows, groups):
    return [r for g in range(groups) for r in range(g, rows, groups)]


ORDER1 = slots_of(R1, 2)
ORDER2 = slots_of(R2, 4)
SLOT2 = {r: s for s, r in enumerate(ORDER2)}


def iota(shape, dim):
    return lax.broadcasted_iota(jnp.int32, shape, dim)


def onehot(mask):
    return jnp.where(mask, 1.0, 0.0).astype(BF)


def dot(a, b):
    return jnp.dot(a, b, preferred_element_type=F32)


def dot_t(a, b):
    return lax.dot_general(a, b, (((1,), (1,)), ((), ())), preferred_element_type=F32)


def send_kernel(dest_ref, cell_ref, traces_ref, out_ref, token_ref):
    dest = dest_ref[...]
    cell = cell_ref[...]
    hot = iota((OWNERS, COUNT), 0) == dest
    upper = onehot(iota((COUNT, COUNT), 0) < iota((COUNT, COUNT), 1))
    before = dot(onehot(hot), upper)
    rank = jnp.sum(jnp.where(hot, before, 0.0), axis=0, keepdims=True)
    place = dest * SLOTS + rank.astype(jnp.int32)
    high = (cell >> 5) + 1
    low = cell & 31
    row = iota((16, COUNT), 0)
    meta = jnp.where(row == 0, high, jnp.where(row == 1, low, 0)).astype(F32).astype(BF)
    traces = traces_ref[...]
    blank = jnp.zeros((EXTRA, TS - SLOTS), F32)
    step = 4
    for o in range(0, OWNERS, step):
        slot = iota((step * SLOTS, COUNT), 0) + o * SLOTS
        placing = onehot(slot == place)
        rows = dot(placing, traces).astype(BF)
        extra = dot_t(meta, placing)
        for k in range(step):
            out_ref[o + k, 0:SLOTS, :] = rows[k * SLOTS : (k + 1) * SLOTS]
            part = extra[0:EXTRA, k * SLOTS : (k + 1) * SLOTS]
            out_ref[o + k, SLOTS:PAY, :] = jnp.concatenate([part, blank], axis=1).astype(BF)
    token_ref[...] = jnp.zeros(token_ref.shape, F32) + rank[:, 0:128]


def weights_kernel(first_ref, mid_ref, last_ref, bias_ref, token_ref, w1_ref, w2_ref, w3_ref, w4_ref):
    bias = 0.5 * bias_ref[...]
    parts = []
    for _ in range(3):
        part = bias.astype(BF)
        parts.append(part)
        bias = bias - part.astype(F32)

    def bias_columns(spread, layer):
        row = iota((16, CH), 0)
        lines = jnp.zeros((16, CH), F32)
        for e in range(3):
            lines = jnp.where(row == e, parts[e][layer : layer + 1].astype(F32), lines)
        spreaded = dot_t(spread, lines.astype(BF)).astype(BF)
        return dot(spreaded, onehot(iota((16, KDIM), 1) == iota((16, KDIM), 0) + TAPS))

    step = 6 * CH
    first = first_ref[...]
    c = iota((step, KDIM), 1)
    b = jnp.where(c >= 80, 1, 0) + jnp.where(c >= 160, 1, 0)
    m = jnp.where(c < TAPS, c - 80 * b, -100)
    ck = iota((9, KDIM), 1)
    bk = jnp.where(ck >= 80, 1, 0) + jnp.where(ck >= 160, 1, 0)
    spread = onehot((iota((step, CH), 0) & (CH - 1)) == iota((step, CH), 1))
    base = dot(spread, first).astype(BF)
    picked = [0.5 * dot(base, onehot(iota((9, KDIM), 0) == 3 * a + bk)) for a in range(3)]
    other = bias_columns(spread, 0)
    for n in range(R1 * CH // step):
        r = (iota((step, KDIM), 0) >> 4) + 6 * n
        r = jnp.where(r < R1 // 2, 2 * r, 2 * r - (R1 - 1))
        total = other
        for a in range(3):
            total = jnp.where(m - r == a, picked[a], total)
        w1_ref[n * step : (n + 1) * step, :] = total.astype(BF)
    rows = GROUP * CH
    spread = onehot((iota((rows, CH), 0) & (CH - 1)) == iota((rows, CH), 1))
    c = iota((rows, KDIM), 1)
    b = jnp.where(c >= 80, 1, 0) + jnp.where(c >= 160, 1, 0)
    delta = jnp.where(c < TAPS, ((c - 80 * b) >> 4) - (iota((rows, KDIM), 0) >> 4), -100)
    ck = iota((144, KDIM), 1)
    bk = jnp.where(ck >= 80, 1, 0) + jnp.where(ck >= 160, 1, 0)
    for layer, out_ref in ((0, w2_ref), (1, w3_ref)):
        base = dot(spread, mid_ref[layer]).astype(BF)
        total = bias_columns(spread, layer + 1)
        for a in range(3):
            pick = onehot(iota((144, KDIM), 0) == (3 * a + bk) * CH + (ck & 15))
            total = jnp.where(delta == a, 0.5 * dot(base, pick), total)
        out_ref[...] = total.astype(BF)
    last = jnp.broadcast_to(last_ref[...], (24, 144))
    delta = (iota((24, 160), 1) >> 4) - (iota((24, 160), 0) & 7)
    tap = iota((24, 160), 0) >> 3
    col = iota((144, 160), 1) & 15
    total = jnp.zeros((24, 160), F32)
    for b in range(3):
        for a in range(3):
            line = dot(last, onehot(iota((144, 160), 0) == (3 * a + b) * CH + col))
            total = jnp.where((delta == a) & (tap == b), line, total)
    w4_ref[...] = total.astype(BF)


def stack_kernel(recv_hbm, w1_ref, pos_ref, out_ref, left_ref, right_ref, recv_ref, sem):
    copy = pltpu.make_async_copy(recv_hbm, recv_ref, sem)
    copy.start()
    copy.wait()
    cells = []
    for s in range(OWNERS):
        extra = recv_ref[s, SLOTS:PAY, 0:SLOTS].astype(F32)
        cells.append((extra[0:1] - 1.0) * 32.0 + extra[1:2])
    cell = jnp.concatenate(cells, axis=1).astype(jnp.int32)
    total = OWNERS * SLOTS
    rows = recv_ref[:, 0:SLOTS, :].reshape(total, TS)
    lefts, rights = [], []
    step = 4
    for c in range(0, CL, step):
        hit = jnp.where(iota((step * MB, total), 0) + c * MB == cell, 1.0, 0.0)
        fold = jnp.maximum(jnp.sum(hit, axis=1, keepdims=True), 1.0)
        part = dot(hit.astype(BF), rows) / fold
        for k in range(step):
            piece = part[k * MB : (k + 1) * MB]
            out_ref[c + k] = piece.astype(BF)
            lefts.append(piece[:, 0:HALO])
            rights.append(piece[:, TS - HALO :])
    left_ref[...] = jnp.concatenate(lefts, axis=1).astype(BF)
    right_ref[...] = jnp.concatenate(rights, axis=1).astype(BF)


def swap_kernel(stack_ref, low_ref, high_ref, out_ref, first_ref, last_ref):
    side = jnp.concatenate([low_ref[...].astype(F32), high_ref[...].astype(F32)], axis=1)
    owner = (iota((MB, TILE), 1) >> 3) & 7
    row = iota((TS + TILE, SEG), 0)
    tau = row + HALO
    tau = jnp.where(row >= TS, row & 7, tau)
    tau = jnp.where(row >= TS + TILE // 2, (row & 7) + TS + HALO, tau)
    col = iota((TS + TILE, SEG), 1)
    order = onehot(tau == TILES * (col & 15) + (col >> 4))
    full = []
    for c in range(CL):
        full.append(jnp.concatenate([stack_ref[c], jnp.where(owner == c, side, 0.0).astype(BF)], axis=1))
    mixed = dot(jnp.concatenate(full, axis=0), order)
    lane = iota((MB, TILE), 1) >> 4
    for k in range(TILES):
        first = (k // 8) * TILE
        tile = jnp.zeros((MB, TILE), F32)
        for c in range(CL):
            block = mixed[c * MB : (c + 1) * MB]
            if first + TILE <= SEG:
                block = block[:, first : first + TILE]
            else:
                block = jnp.concatenate([block[:, first:SEG], jnp.zeros((MB, first + TILE - SEG), F32)], axis=1)
            shift = 16 * ((c - k) % 8)
            if shift:
                block = pltpu.roll(block, shift, 1)
            tile = jnp.where(lane == c, block, tile)
        tile = tile.astype(BF)
        out_ref[:, k * TILE : (k + 1) * TILE] = tile
    first_ref[...] = out_ref[0:HALO, :]
    last_ref[...] = out_ref[MB - HALO : MB, :]


def gelu_half(h):
    c0 = 2.0 * 0.7978845608028654
    c1 = 8.0 * 0.7978845608028654 * 0.044715
    return h + h * jnp.tanh(h * (c0 + c1 * (h * h)))


def turned(block, shift):
    return pltpu.roll(block.astype(F32), shift % TILE, 1).astype(BF)


def conv_kernel(pos_ref, core_ref, low_ref, high_ref, stack_ref, w1_ref, w2_ref, w3_ref, w4_ref, out_ref,
                x_ref, h1_ref, h2_ref, h3_ref, p_ref, mask_ref):
    mid = pos_ref[0]
    tm = pos_ref[1]
    lane = iota((CH, WIDE), 1)
    t = TILES * ((lane & 127) & 15) + (lane >> 7) - HALO + tm * TS
    keep = jnp.where((t >= 0) & (t < 4 * TS), 1.0, 0.0)
    mask_ref[0] = keep.astype(BF)
    mask_ref[1] = (keep * jnp.where(mid > 0, 1.0, 0.0)).astype(BF)
    mask_ref[2] = (keep * jnp.where(mid < 7, 1.0, 0.0)).astype(BF)

    def at(k):
        return slice((LEAD + k) * TILE, (LEAD + k + 1) * TILE)

    image = jnp.concatenate([low_ref[...].astype(F32), core_ref[...].astype(F32), high_ref[...].astype(F32)], axis=0)
    x_ref[:, TILE : TILE + LANES] = image.astype(BF)
    x_ref[:, 0:TILE] = pltpu.roll(image[:, 16 * TILE :], 1, 1).astype(BF)
    for k in range(2):
        x_ref[:, (18 + k) * TILE : (19 + k) * TILE] = pltpu.roll(image[:, k * TILE : (k + 1) * TILE], TILE - 1, 1).astype(BF)
    ones = jnp.ones((KDIM - TAPS, CHUNK), BF)
    h1_ref[R1 * CH :, :] = jnp.zeros((2 * CH, EXT), BF)
    h1_ref[:, (LEAD + 19) * TILE :] = jnp.zeros((80 * CH, 3 * TILE), BF)
    h2_ref[:, (LEAD + 21) * TILE :] = jnp.zeros((R2 * CH, TILE), BF)

    def finish(acc, row, base, into_ref, slot, lead):
        which = 1 if row < 0 else (2 if row >= MB else 0)
        g = gelu_half(acc).astype(BF) * mask_ref[which, :, pl.ds(base, CHUNK)]
        into_ref[slot * CH : (slot + 1) * CH, pl.ds(pl.multiple_of(base + lead * TILE, TILE), CHUNK)] = g

    def layer1(n, _):
        base = pl.multiple_of(n * CHUNK, CHUNK)
        x = [x_ref[:, pl.ds(pl.multiple_of(base + b * TILE, TILE), CHUNK)] for b in range(3)]
        x = jnp.concatenate(x + [ones], axis=0)
        for s0 in range(0, R1, 13):
            acc = dot(w1_ref[s0 * CH : (s0 + 13) * CH, :], x)
            for j in range(13):
                finish(acc[j * CH : (j + 1) * CH], ORDER1[s0 + j] - 7, base, h1_ref, s0 + j, LEAD)
        return 0

    lax.fori_loop(0, NCHUNK, layer1, 0)
    for k in range(2):
        h1_ref[: R1 * CH, at(TILES + k)] = turned(h1_ref[: R1 * CH, at(k)], -1)
        h1_ref[: R1 * CH, at(-1 - k)] = turned(h1_ref[: R1 * CH, at(TILES - 1 - k)], 1)

    def window(ref, s0, base, d):
        taps = [
            ref[s0 * CH : (s0 + 5) * CH, pl.ds(pl.multiple_of(base + (LEAD + (b - 1) * d) * TILE, TILE), CHUNK)]
            for b in range(3)
        ]
        return jnp.concatenate(taps + [ones], axis=0)

    def layer2(n, _):
        base = pl.multiple_of(n * CHUNK, CHUNK)
        for s0 in range(0, R1 - 2, GROUP):
            acc = dot(w2_ref[...], window(h1_ref, s0, base, 2))
            for j in range(GROUP):
                if s0 + j < R1 and ORDER1[s0 + j] < R2:
                    q = ORDER1[s0 + j]
                    finish(acc[j * CH : (j + 1) * CH], q - 5, base, h2_ref, SLOT2[q], LEAD)
        return 0

    lax.fori_loop(0, NCHUNK, layer2, 0)
    for k in range(4):
        h2_ref[:, at(TILES + k)] = turned(h2_ref[:, at(k)], -1)
        h2_ref[:, at(-1 - k)] = turned(h2_ref[:, at(TILES - 1 - k)], 1)

    def layer3(n, _):
        base = pl.multiple_of(n * CHUNK, CHUNK)
        for s0 in range(0, R2 - 2, GROUP):
            acc = dot(w3_ref[...], window(h2_ref, s0, base, 4))
            for j in range(GROUP):
                if ORDER2[s0 + j] < R3:
                    q = ORDER2[s0 + j]
                    finish(acc[j * CH : (j + 1) * CH], q - 1, base, h3_ref, q, 0)
        for q in range(0, MB, 8):
            acc = dot(w4_ref[...], h3_ref[q * CH : (q + 10) * CH, pl.ds(base, CHUNK)])
            for b in range(3):
                p_ref[b, q : q + 8, pl.ds(pl.multiple_of(base + TILE, TILE), CHUNK)] = acc[8 * b : 8 * b + 8]
        return 0

    lax.fori_loop(0, NCHUNK, layer3, 0)
    p_ref[0, :, 0:TILE] = pltpu.roll(p_ref[0, :, TILES * TILE : (TILES + 1) * TILE], 1, 1)
    p_ref[2, :, (TILES + 1) * TILE : (TILES + 2) * TILE] = pltpu.roll(p_ref[2, :, TILE : 2 * TILE], TILE - 1, 1)
    tiles = [
        p_ref[0, :, k * TILE : (k + 1) * TILE]
        + p_ref[1, :, (k + 1) * TILE : (k + 2) * TILE]
        + p_ref[2, :, (k + 2) * TILE : (k + 3) * TILE]
        for k in range(TILES)
    ]
    col = iota((3 * TILE, TS), 0)
    order = onehot((TILES * (col & 15) + (col >> 4) == iota((3 * TILE, TS), 1) + HALO) & (col < SEG))
    group = iota((MB, TILE), 1) >> 4
    for c in range(CL):
        parts = []
        for first in range(0, 24, 8):
            block = jnp.zeros((MB, TILE), F32)
            for k in range(first, min(first + 8, TILES)):
                shift = 16 * ((k - c) % 8)
                block = jnp.where(group == k % 8, pltpu.roll(tiles[k], shift, 1) if shift else tiles[k], block)
            parts.append(block)
        noise = jnp.concatenate(parts, axis=1)
        top = noise.astype(BF)
        rest = (noise - top.astype(F32)).astype(BF)
        out_ref[c] = stack_ref[c].astype(F32) - (dot(top, order) + dot(rest, order))


def call(kernel, outs, scratch=(), smem=0, n=0, loose=0, name=None):
    specs = [pl.BlockSpec(memory_space=pltpu.SMEM) for _ in range(smem)]
    specs += [pl.BlockSpec(memory_space=pltpu.VMEM) for _ in range(n)]
    specs += [pl.BlockSpec(memory_space=pl.ANY) for _ in range(loose)]
    return pl.pallas_call(
        kernel,
        out_shape=outs,
        in_specs=specs,
        out_specs=jax.tree.map(lambda _: pl.BlockSpec(memory_space=pltpu.VMEM), outs),
        scratch_shapes=list(scratch),
        compiler_params=pltpu.CompilerParams(vmem_limit_bytes=60000 * 1024),
        name=name,
    )


def shape(*dims, dtype=BF):
    return jax.ShapeDtypeStruct(dims, dtype)


def build_send(dest, cell, traces):
    return call(send_kernel, (shape(OWNERS, PAY, TS), shape(8, 128, dtype=F32)), n=3, name="send")(dest, cell, traces)


def build_weights(w_first, w_mid, w_last, bias, token):
    outs = (shape(R1 * CH, KDIM), shape(GROUP * CH, KDIM), shape(GROUP * CH, KDIM), shape(24, 160))
    return call(weights_kernel, outs, n=5, name="weights")(w_first, w_mid, w_last, bias, token)


def build_stack(recv, w1, pos):
    outs = (shape(CL, MB, TS), shape(MB, MB), shape(MB, MB))
    scratch = [pltpu.VMEM((OWNERS, PAY, TS), BF), pltpu.SemaphoreType.DMA]
    return call(stack_kernel, outs, scratch, loose=3, name="stack")(recv, w1, pos)


def reorder(stack, low, high):
    outs = (shape(MB, LANES), shape(HALO, LANES), shape(HALO, LANES))
    return call(swap_kernel, outs, n=3, name="reorder")(stack, low, high)


def convolve(pos, core, low, high, stack, weights):
    scratch = [
        pltpu.VMEM((80, 20 * TILE), BF),
        pltpu.VMEM((80 * CH, EXT), BF),
        pltpu.VMEM((R2 * CH, EXT), BF),
        pltpu.VMEM((R3 * CH, WIDE), BF),
        pltpu.VMEM((3, MB, 20 * TILE), F32),
        pltpu.VMEM((3, CH, WIDE), BF),
    ]
    return call(conv_kernel, shape(CL, MB, TS, dtype=F32), scratch, smem=1, n=8, name="conv")(
        pos, core, low, high, stack, *weights
    )


def neighbours(low_edge, high_edge, axis):
    count = lax.axis_size(axis)
    up = [(i, i + 1) for i in range(count - 1)]
    down = [(b, a) for a, b in up]
    return lax.ppermute(high_edge, axis, up), lax.ppermute(low_edge, axis, down)


def shards(traces, dest, cell, w_first, w_mid, w_last, bias):
    send, token = build_send(dest.reshape(1, COUNT), cell.reshape(1, COUNT), traces)
    recv = lax.all_to_all(send, ("offset", "mid"), split_axis=0, concat_axis=0, tiled=True)
    weights = build_weights(w_first, w_mid, w_last, bias, token)
    pos = jnp.stack([lax.axis_index("mid"), lax.axis_index("tm")]).astype(jnp.int32)
    stack, left, right = build_stack(recv, weights[0], pos)
    low, high = neighbours(left, right, "tm")
    core, first, last = reorder(stack, low, high)
    below, above = neighbours(first, last, "mid")
    return convolve(pos, core, below, above, stack, weights)


def solution(mesh):
    rows = P(("offset", "mid"), "tm")
    column = P(("offset", "mid"), None)
    placed = (rows, column, column, P(), P(), P(), P())
    return jax.shard_map(
        shards, mesh=mesh, in_specs=placed, out_specs=P("offset", "mid", "tm"), check_vma=False
    )
```

```python
import functools

import jax
import jax.numpy as jnp
from jax import lax
from jax.experimental import pallas as pl
from jax.experimental.pallas import tpu as pltpu
from jax.sharding import PartitionSpec as P

BF = jnp.bfloat16
F32 = jnp.float32
OWNERS = 32
SLOTS = 64
COUNT = 1024
TS = 256
CL = 8
MB = 64
HALO = 8
SEG = TS + 2 * HALO
LANES = CL * SEG
TILE = 128
TILES = 17
CHUNK = 2 * TILE
NCHUNK = 9
WIDE = CHUNK * NCHUNK
LEAD = 4
EXT = (LEAD + 22) * TILE
CH = 16
R1, R2, R3 = 78, 74, 66
TAPS = 240
KDIM = 256
GROUP = 3
U1, U2, U3 = 3, 3, 3
EXTRA = 8
PAY = SLOTS + EXTRA


def slots_of(rows, groups):
    return [r for g in range(groups) for r in range(g, rows, groups)]


ORDER1 = slots_of(R1, 2)
ORDER2 = slots_of(R2, 4)
SLOT2 = {r: s for s, r in enumerate(ORDER2)}


def iota(shape, dim):
    return lax.broadcasted_iota(jnp.int32, shape, dim)


def onehot(mask):
    return jnp.where(mask, 1.0, 0.0).astype(BF)


def dot(a, b):
    return jnp.dot(a, b, preferred_element_type=F32)


def dot_t(a, b):
    return lax.dot_general(a, b, (((1,), (1,)), ((), ())), preferred_element_type=F32)


def send_kernel(dest_ref, cell_ref, traces_ref, out_ref, token_ref):
    dest = dest_ref[...]
    cell = cell_ref[...]
    width = 256
    blocks = COUNT // width
    owner = iota((OWNERS, width), 0)
    hots = [owner == dest[:, n * width : (n + 1) * width] for n in range(blocks)]
    upper = onehot(iota((width, width), 0) < iota((width, width), 1))
    before = dot(jnp.concatenate([onehot(hot) for hot in hots], axis=0), upper)
    ranks = []
    offset = jnp.zeros((OWNERS, 1), F32)
    for n, hot in enumerate(hots):
        part = before[n * OWNERS : (n + 1) * OWNERS]
        ranks.append(jnp.sum(jnp.where(hot, part + offset, 0.0), axis=0, keepdims=True))
        offset = offset + jnp.sum(jnp.where(hot, 1.0, 0.0), axis=1, keepdims=True)
    rank = jnp.concatenate(ranks, axis=1)
    place = dest * SLOTS + rank.astype(jnp.int32)
    high = (cell >> 5) + 1
    low = cell & 31
    row = iota((16, COUNT), 0)
    meta = jnp.where(row == 0, high, jnp.where(row == 1, low, 0)).astype(F32).astype(BF)
    traces = traces_ref[...]
    blank = jnp.zeros((EXTRA, TS - SLOTS), F32)
    step = 8
    for o in range(0, OWNERS, step):
        slot = iota((step * SLOTS, COUNT), 0) + o * SLOTS
        placing = onehot(slot == place)
        rows = dot(placing, traces).astype(BF)
        extra = dot_t(meta, placing)
        for k in range(step):
            out_ref[o + k, 0:SLOTS, :] = rows[k * SLOTS : (k + 1) * SLOTS]
            part = extra[0:EXTRA, k * SLOTS : (k + 1) * SLOTS]
            out_ref[o + k, SLOTS:PAY, :] = jnp.concatenate([part, blank], axis=1).astype(BF)
    token_ref[...] = jnp.zeros(token_ref.shape, F32) + rank[:, 0:128]


def weights_kernel(first_ref, mid_ref, last_ref, bias_ref, token_ref, w1_ref, w2_ref, w3_ref, w4_ref):
    bias = 0.5 * bias_ref[...]
    parts = []
    for _ in range(3):
        part = bias.astype(BF)
        parts.append(part)
        bias = bias - part.astype(F32)

    def bias_columns(spread, layer):
        row = iota((16, CH), 0)
        lines = jnp.zeros((16, CH), F32)
        for e in range(3):
            lines = jnp.where(row == e, parts[e][layer : layer + 1].astype(F32), lines)
        spreaded = dot_t(spread, lines.astype(BF)).astype(BF)
        return dot(spreaded, onehot(iota((16, KDIM), 1) == iota((16, KDIM), 0) + TAPS))

    step = 6 * CH
    first = first_ref[...]
    c = iota((step, KDIM), 1)
    b = jnp.where(c >= 80, 1, 0) + jnp.where(c >= 160, 1, 0)
    m = jnp.where(c < TAPS, c - 80 * b, -100)
    ck = iota((9, KDIM), 1)
    bk = jnp.where(ck >= 80, 1, 0) + jnp.where(ck >= 160, 1, 0)
    spread = onehot((iota((step, CH), 0) & (CH - 1)) == iota((step, CH), 1))
    base = dot(spread, first).astype(BF)
    picked = [0.5 * dot(base, onehot(iota((9, KDIM), 0) == 3 * a + bk)) for a in range(3)]
    other = bias_columns(spread, 0)
    for n in range(R1 * CH // step):
        r = (iota((step, KDIM), 0) >> 4) + 6 * n
        r = jnp.where(r < R1 // 2, 2 * r, 2 * r - (R1 - 1))
        total = other
        for a in range(3):
            total = jnp.where(m - r == a, picked[a], total)
        w1_ref[n * step : (n + 1) * step, :] = total.astype(BF)
    rows = GROUP * CH
    spread = onehot((iota((rows, CH), 0) & (CH - 1)) == iota((rows, CH), 1))
    c = iota((rows, KDIM), 1)
    b = jnp.where(c >= 80, 1, 0) + jnp.where(c >= 160, 1, 0)
    delta = jnp.where(c < TAPS, ((c - 80 * b) >> 4) - (iota((rows, KDIM), 0) >> 4), -100)
    ck = iota((144, KDIM), 1)
    bk = jnp.where(ck >= 80, 1, 0) + jnp.where(ck >= 160, 1, 0)
    for layer, out_ref in ((0, w2_ref), (1, w3_ref)):
        base = dot(spread, mid_ref[layer]).astype(BF)
        total = bias_columns(spread, layer + 1)
        for a in range(3):
            pick = onehot(iota((144, KDIM), 0) == (3 * a + bk) * CH + (ck & 15))
            total = jnp.where(delta == a, 0.5 * dot(base, pick), total)
        out_ref[...] = total.astype(BF)
    last = jnp.broadcast_to(last_ref[...], (24, 144))
    delta = (iota((24, 160), 1) >> 4) - (iota((24, 160), 0) & 7)
    tap = iota((24, 160), 0) >> 3
    col = iota((144, 160), 1) & 15
    total = jnp.zeros((24, 160), F32)
    for b in range(3):
        for a in range(3):
            line = dot(last, onehot(iota((144, 160), 0) == (3 * a + b) * CH + col))
            total = jnp.where((delta == a) & (tap == b), line, total)
    w4_ref[...] = total.astype(BF)


def stack_kernel(recv_ref, w1_ref, pos_ref, out_ref, left_ref, right_ref):
    cells = []
    for s in range(OWNERS):
        extra = recv_ref[s, SLOTS:PAY, 0:SLOTS].astype(F32)
        cells.append((extra[0:1] - 1.0) * 32.0 + extra[1:2])
    cell = jnp.concatenate(cells, axis=1).astype(jnp.int32)
    total = OWNERS * SLOTS
    rows = recv_ref[:, 0:SLOTS, :].reshape(total, TS)
    lefts, rights = [], []
    step = 4
    for c in range(0, CL, step):
        hit = jnp.where(iota((step * MB, total), 0) + c * MB == cell, 1.0, 0.0)
        fold = jnp.maximum(jnp.sum(hit, axis=1, keepdims=True), 1.0)
        part = dot(hit.astype(BF), rows) / fold
        for k in range(step):
            piece = part[k * MB : (k + 1) * MB]
            out_ref[c + k] = piece.astype(BF)
            lefts.append(piece[:, 0:HALO])
            rights.append(piece[:, TS - HALO :])
    left_ref[...] = jnp.concatenate(lefts, axis=1).astype(BF)
    right_ref[...] = jnp.concatenate(rights, axis=1).astype(BF)


def transposed(blocks):
    group = iota(blocks[0].shape, 1) >> 4
    blocks = list(blocks)
    for bit in (1, 2, 4):
        keep = (group & bit) == 0
        for i in range(8):
            if i & bit == 0:
                a, b = blocks[i], blocks[i | bit]
                blocks[i] = jnp.where(keep, a, pltpu.roll(b, 16 * bit, 1))
                blocks[i | bit] = jnp.where(keep, pltpu.roll(a, TILE - 16 * bit, 1), b)
    return blocks


def swap_kernel(stack_ref, low_ref, high_ref, out_ref, first_ref, last_ref):
    side = jnp.concatenate([low_ref[...].astype(F32), high_ref[...].astype(F32)], axis=1)
    owner = (iota((MB, TILE), 1) >> 3) & 7
    rows = TS + TILE
    row = iota((rows, 1), 0)
    tau = row + HALO
    tau = jnp.where(row >= TS, row & 7, tau)
    tau = jnp.where(row >= TS + TILE // 2, (row & 7) + TS + HALO, tau)
    col = iota((1, 3 * TILE), 1)
    order = onehot(tau == TILES * (col & 15) + jnp.minimum(col >> 4, TILES - 1))
    full = []
    for c in range(CL):
        full.append(jnp.concatenate([stack_ref[c], jnp.where(owner == c, side, 0.0).astype(BF)], axis=1))
    mixed = dot(jnp.concatenate(full, axis=0), order)
    for half in range(2):
        blocks = [mixed[c * MB : (c + 1) * MB, half * TILE : (half + 1) * TILE] for c in range(CL)]
        for k, tile in enumerate(transposed(blocks)):
            k = 8 * half + k
            out_ref[:, k * TILE : (k + 1) * TILE] = tile.astype(BF)
    lane = iota((MB, TILE), 1) >> 4
    tile = jnp.zeros((MB, TILE), F32)
    for c in range(CL):
        tile = jnp.where(lane == c, mixed[c * MB : (c + 1) * MB, 2 * TILE :], tile)
    out_ref[:, 16 * TILE :] = tile.astype(BF)
    first_ref[...] = out_ref[0:HALO, :]
    last_ref[...] = out_ref[MB - HALO : MB, :]


def gelu_half(h):
    c0 = 2.0 * 0.7978845608028654
    c1 = 8.0 * 0.7978845608028654 * 0.044715
    return h + h * jnp.tanh(h * (c0 + c1 * (h * h)))


def turned(block, shift):
    return pltpu.roll(block, shift % TILE, 1)


def sweep(layer, unroll):
    def step(n, _):
        start = pl.multiple_of(n * (unroll * CHUNK), unroll * CHUNK)
        for k in range(unroll):
            layer(start, k * CHUNK)
        return 0

    lax.fori_loop(0, NCHUNK // unroll, step, 0)


def conv_kernel(pos_ref, core_ref, low_ref, high_ref, stack_ref, w1_ref, w2_ref, w3_ref, w4_ref, out_ref,
                x_ref, h1_ref, h2_ref, h3_ref, p_ref, mask_ref):
    mid = pos_ref[0]
    tm = pos_ref[1]
    lane = iota((CH, WIDE), 1)
    t = TILES * ((lane & 127) & 15) + (lane >> 7) - HALO + tm * TS
    keep = jnp.where((t >= 0) & (t < 4 * TS), 1.0, 0.0)
    mask_ref[0] = keep.astype(BF)
    mask_ref[1] = (keep * jnp.where(mid > 0, 1.0, 0.0)).astype(BF)
    mask_ref[2] = (keep * jnp.where(mid < 7, 1.0, 0.0)).astype(BF)

    def at(k):
        return slice((LEAD + k) * TILE, (LEAD + k + 1) * TILE)

    image = jnp.concatenate([low_ref[...].astype(F32), core_ref[...].astype(F32), high_ref[...].astype(F32)], axis=0)
    x_ref[:, TILE : TILE + LANES] = image.astype(BF)
    x_ref[:, 0:TILE] = pltpu.roll(image[:, 16 * TILE :], 1, 1).astype(BF)
    for k in range(2):
        x_ref[:, (18 + k) * TILE : (19 + k) * TILE] = pltpu.roll(image[:, k * TILE : (k + 1) * TILE], TILE - 1, 1).astype(BF)
    ones = jnp.ones((KDIM - TAPS, CHUNK), BF)
    h1_ref[R1 * CH :, :] = jnp.zeros((2 * CH, EXT), BF)
    h1_ref[:, (LEAD + 19) * TILE :] = jnp.zeros((80 * CH, 3 * TILE), BF)
    h2_ref[:, (LEAD + 21) * TILE :] = jnp.zeros((R2 * CH, TILE), BF)

    def finish(acc, row, base, into_ref, slot, lead):
        which = 1 if row < 0 else (2 if row >= MB else 0)
        g = gelu_half(acc).astype(BF) * mask_ref[which, :, pl.ds(pl.multiple_of(base, CHUNK), CHUNK)]
        into_ref[slot * CH : (slot + 1) * CH, pl.ds(pl.multiple_of(base + lead * TILE, TILE), CHUNK)] = g

    def layer1(start, step):
        base = start + step
        x = [x_ref[:, pl.ds(pl.multiple_of(base + b * TILE, TILE), CHUNK)] for b in range(3)]
        x = jnp.concatenate(x + [ones], axis=0)
        for s0 in range(0, R1, 13):
            acc = dot(w1_ref[s0 * CH : (s0 + 13) * CH, :], x)
            for j in range(13):
                finish(acc[j * CH : (j + 1) * CH], ORDER1[s0 + j] - 7, base, h1_ref, s0 + j, LEAD)

    sweep(layer1, U1)
    for k in range(2):
        h1_ref[: R1 * CH, at(TILES + k)] = turned(h1_ref[: R1 * CH, at(k)], -1)
        h1_ref[: R1 * CH, at(-1 - k)] = turned(h1_ref[: R1 * CH, at(TILES - 1 - k)], 1)

    def window(ref, s0, base, d):
        taps = [
            ref[s0 * CH : (s0 + 5) * CH, pl.ds(pl.multiple_of(base + (LEAD + (b - 1) * d) * TILE, TILE), CHUNK)]
            for b in range(3)
        ]
        return jnp.concatenate(taps + [ones], axis=0)

    def layer2(start, step):
        base = start + step
        for s0 in range(0, R1 - 2, GROUP):
            acc = dot(w2_ref[...], window(h1_ref, s0, base, 2))
            for j in range(GROUP):
                if s0 + j < R1 and ORDER1[s0 + j] < R2:
                    q = ORDER1[s0 + j]
                    finish(acc[j * CH : (j + 1) * CH], q - 5, base, h2_ref, SLOT2[q], LEAD)

    sweep(layer2, U2)
    for k in range(4):
        h2_ref[:, at(TILES + k)] = turned(h2_ref[:, at(k)], -1)
        h2_ref[:, at(-1 - k)] = turned(h2_ref[:, at(TILES - 1 - k)], 1)

    def layer3(start, step):
        base = start + step
        for s0 in range(0, R2 - 2, GROUP):
            acc = dot(w3_ref[...], window(h2_ref, s0, base, 4))
            for j in range(GROUP):
                if ORDER2[s0 + j] < R3:
                    q = ORDER2[s0 + j]
                    finish(acc[j * CH : (j + 1) * CH], q - 1, base, h3_ref, q, 0)
        for q in range(0, MB, 8):
            acc = dot(w4_ref[...], h3_ref[q * CH : (q + 10) * CH, pl.ds(pl.multiple_of(base, CHUNK), CHUNK)])
            for b in range(3):
                p_ref[b, q : q + 8, pl.ds(pl.multiple_of(base + TILE, TILE), CHUNK)] = acc[8 * b : 8 * b + 8]

    sweep(layer3, U3)
    p_ref[0, :, 0:TILE] = pltpu.roll(p_ref[0, :, TILES * TILE : (TILES + 1) * TILE], 1, 1)
    p_ref[2, :, (TILES + 1) * TILE : (TILES + 2) * TILE] = pltpu.roll(p_ref[2, :, TILE : 2 * TILE], TILE - 1, 1)
    tiles = [
        p_ref[0, :, k * TILE : (k + 1) * TILE]
        + p_ref[1, :, (k + 1) * TILE : (k + 2) * TILE]
        + p_ref[2, :, (k + 2) * TILE : (k + 3) * TILE]
        for k in range(TILES)
    ]
    col = iota((3 * TILE, 1), 0)
    tau = jnp.where(col < SEG, TILES * (col & 15) + (col >> 4), -1)
    order = onehot(tau == iota((1, TS), 1) + HALO)
    firsts, seconds = transposed(tiles[0:8]), transposed(tiles[8:16])
    for c in range(CL):
        third = pltpu.roll(tiles[16], TILE - 16 * c, 1) if c else tiles[16]
        noise = jnp.concatenate([firsts[c], seconds[c], third], axis=1)
        top = noise.astype(BF)
        rest = (noise - top.astype(F32)).astype(BF)
        both = dot(jnp.concatenate([top, rest], axis=0), order)
        out_ref[c] = stack_ref[c].astype(F32) - (both[0:MB] + both[MB:])


def call(kernel, outs, scratch=(), smem=0, n=0, loose=0, name=None):
    specs = [pl.BlockSpec(memory_space=pltpu.SMEM) for _ in range(smem)]
    specs += [pl.BlockSpec(memory_space=pltpu.VMEM) for _ in range(n)]
    specs += [pl.BlockSpec(memory_space=pl.ANY) for _ in range(loose)]
    return pl.pallas_call(
        kernel,
        out_shape=outs,
        in_specs=specs,
        out_specs=jax.tree.map(lambda _: pl.BlockSpec(memory_space=pltpu.VMEM), outs),
        scratch_shapes=list(scratch),
        compiler_params=pltpu.CompilerParams(vmem_limit_bytes=60000 * 1024),
        name=name,
    )


def shape(*dims, dtype=BF):
    return jax.ShapeDtypeStruct(dims, dtype)


def near(x):
    return pltpu.with_memory_space_constraint(x, pltpu.VMEM)


def build_send(dest, cell, traces):
    return call(send_kernel, (shape(OWNERS, PAY, TS), shape(8, 128, dtype=F32)), n=3, name="send")(dest, cell, traces)


def build_weights(w_first, w_mid, w_last, bias, token):
    outs = (shape(R1 * CH, KDIM), shape(GROUP * CH, KDIM), shape(GROUP * CH, KDIM), shape(24, 160))
    return call(weights_kernel, outs, n=5, name="weights")(w_first, w_mid, w_last, bias, token)


def build_stack(recv, w1, pos):
    outs = (shape(CL, MB, TS), shape(MB, MB), shape(MB, MB))
    return call(stack_kernel, outs, n=1, loose=2, name="stack")(near(recv), w1, pos)


def reorder(stack, low, high):
    outs = (shape(MB, LANES), shape(HALO, LANES), shape(HALO, LANES))
    return call(swap_kernel, outs, n=3, name="reorder")(stack, near(low), near(high))


def convolve(pos, core, low, high, stack, weights):
    scratch = [
        pltpu.VMEM((80, 20 * TILE), BF),
        pltpu.VMEM((80 * CH, EXT), BF),
        pltpu.VMEM((R2 * CH, EXT), BF),
        pltpu.VMEM((R3 * CH, WIDE), BF),
        pltpu.VMEM((3, MB, 20 * TILE), F32),
        pltpu.VMEM((3, CH, WIDE), BF),
    ]
    return call(conv_kernel, shape(CL, MB, TS, dtype=F32), scratch, smem=1, n=8, name="conv")(
        pos, core, near(low), near(high), stack, *weights
    )


def neighbours(low_edge, high_edge, axis):
    count = lax.axis_size(axis)
    up = [(i, i + 1) for i in range(count - 1)]
    down = [(b, a) for a, b in up]
    return lax.ppermute(high_edge, axis, up), lax.ppermute(low_edge, axis, down)


def shards(traces, dest, cell, w_first, w_mid, w_last, bias):
    send, token = build_send(dest.reshape(1, COUNT), cell.reshape(1, COUNT), traces)
    recv = lax.all_to_all(send, ("offset", "mid"), split_axis=0, concat_axis=0, tiled=True)
    weights = build_weights(w_first, w_mid, w_last, bias, token)
    pos = jnp.stack([lax.axis_index("mid"), lax.axis_index("tm")]).astype(jnp.int32)
    stack, left, right = build_stack(recv, weights[0], pos)
    low, high = neighbours(left, right, "tm")
    core, first, last = reorder(stack, low, high)
    below, above = neighbours(first, last, "mid")
    return convolve(pos, core, below, above, stack, weights)


def solution(mesh):
    rows = P(("offset", "mid"), "tm")
    column = P(("offset", "mid"), None)
    placed = (rows, column, column, P(), P(), P(), P())
    return jax.shard_map(
        shards, mesh=mesh, in_specs=placed, out_specs=P("offset", "mid", "tm"), check_vma=False
    )
```

```python
import functools

import jax
import jax.numpy as jnp
from jax import lax
from jax.experimental import pallas as pl
from jax.experimental.pallas import tpu as pltpu
from jax.sharding import PartitionSpec as P

BF = jnp.bfloat16
F32 = jnp.float32
OWNERS = 32
SLOTS = 64
COUNT = 1024
TS = 256
CL = 8
MB = 64
HALO = 8
SEG = TS + 2 * HALO
LANES = CL * SEG
TILE = 128
TILES = 17
CHUNK = 2 * TILE
NCHUNK = 9
WIDE = CHUNK * NCHUNK
LEAD = 4
EXT = (LEAD + 22) * TILE
CH = 16
R1, R2, R3 = 78, 74, 66
TAPS = 240
KDIM = 256
GROUP = 3
EXTRA = 8
PAY = SLOTS + EXTRA


def slots_of(rows, groups):
    return [r for g in range(groups) for r in range(g, rows, groups)]


ORDER1 = slots_of(R1, 2)
ORDER2 = slots_of(R2, 4)
SLOT2 = {r: s for s, r in enumerate(ORDER2)}


def iota(shape, dim):
    return lax.broadcasted_iota(jnp.int32, shape, dim)


def onehot(mask):
    return jnp.where(mask, 1.0, 0.0).astype(BF)


def dot(a, b):
    return jnp.dot(a, b, preferred_element_type=F32)


def dot_t(a, b):
    return lax.dot_general(a, b, (((1,), (1,)), ((), ())), preferred_element_type=F32)


def send_kernel(dest_ref, cell_ref, traces_ref, out_ref, token_ref):
    dest = dest_ref[...]
    cell = cell_ref[...]
    width = 256
    blocks = COUNT // width
    owner = iota((OWNERS, width), 0)
    hots = [owner == dest[:, n * width : (n + 1) * width] for n in range(blocks)]
    upper = onehot(iota((width, width), 0) < iota((width, width), 1))
    before = dot(jnp.concatenate([onehot(hot) for hot in hots], axis=0), upper)
    ranks = []
    offset = jnp.zeros((OWNERS, 1), F32)
    for n, hot in enumerate(hots):
        part = before[n * OWNERS : (n + 1) * OWNERS]
        ranks.append(jnp.sum(jnp.where(hot, part + offset, 0.0), axis=0, keepdims=True))
        offset = offset + jnp.sum(jnp.where(hot, 1.0, 0.0), axis=1, keepdims=True)
    rank = jnp.concatenate(ranks, axis=1)
    place = dest * SLOTS + rank.astype(jnp.int32)
    high = (cell >> 5) + 1
    low = cell & 31
    row = iota((16, COUNT), 0)
    meta = jnp.where(row == 0, high, jnp.where(row == 1, low, 0)).astype(F32).astype(BF)
    traces = traces_ref[...]
    blank = jnp.zeros((EXTRA, TS - SLOTS), F32)
    step = 8
    for o in range(0, OWNERS, step):
        slot = iota((step * SLOTS, COUNT), 0) + o * SLOTS
        placing = onehot(slot == place)
        rows = dot(placing, traces).astype(BF)
        extra = dot_t(meta, placing)
        for k in range(step):
            out_ref[o + k, 0:SLOTS, :] = rows[k * SLOTS : (k + 1) * SLOTS]
            part = extra[0:EXTRA, k * SLOTS : (k + 1) * SLOTS]
            out_ref[o + k, SLOTS:PAY, :] = jnp.concatenate([part, blank], axis=1).astype(BF)
    token_ref[...] = jnp.zeros(token_ref.shape, F32) + rank[:, 0:128]


def weights_kernel(first_ref, mid_ref, last_ref, bias_ref, token_ref, w1_ref, w2_ref, w3_ref, w4_ref):
    bias = 0.5 * bias_ref[...]
    parts = []
    for _ in range(3):
        part = bias.astype(BF)
        parts.append(part)
        bias = bias - part.astype(F32)

    def bias_columns(spread, layer):
        row = iota((16, CH), 0)
        lines = jnp.zeros((16, CH), F32)
        for e in range(3):
            lines = jnp.where(row == e, parts[e][layer : layer + 1].astype(F32), lines)
        spreaded = dot_t(spread, lines.astype(BF)).astype(BF)
        return dot(spreaded, onehot(iota((16, KDIM), 1) == iota((16, KDIM), 0) + TAPS))

    step = 6 * CH
    first = first_ref[...]
    c = iota((step, KDIM), 1)
    b = jnp.where(c >= 80, 1, 0) + jnp.where(c >= 160, 1, 0)
    m = jnp.where(c < TAPS, c - 80 * b, -100)
    ck = iota((9, KDIM), 1)
    bk = jnp.where(ck >= 80, 1, 0) + jnp.where(ck >= 160, 1, 0)
    spread = onehot((iota((step, CH), 0) & (CH - 1)) == iota((step, CH), 1))
    base = dot(spread, first).astype(BF)
    picked = [0.5 * dot(base, onehot(iota((9, KDIM), 0) == 3 * a + bk)) for a in range(3)]
    other = bias_columns(spread, 0)
    for n in range(R1 * CH // step):
        r = (iota((step, KDIM), 0) >> 4) + 6 * n
        r = jnp.where(r < R1 // 2, 2 * r, 2 * r - (R1 - 1))
        total = other
        for a in range(3):
            total = jnp.where(m - r == a, picked[a], total)
        w1_ref[n * step : (n + 1) * step, :] = total.astype(BF)
    rows = GROUP * CH
    spread = onehot((iota((rows, CH), 0) & (CH - 1)) == iota((rows, CH), 1))
    c = iota((rows, KDIM), 1)
    b = jnp.where(c >= 80, 1, 0) + jnp.where(c >= 160, 1, 0)
    delta = jnp.where(c < TAPS, ((c - 80 * b) >> 4) - (iota((rows, KDIM), 0) >> 4), -100)
    ck = iota((144, KDIM), 1)
    bk = jnp.where(ck >= 80, 1, 0) + jnp.where(ck >= 160, 1, 0)
    for layer, out_ref in ((0, w2_ref), (1, w3_ref)):
        base = dot(spread, mid_ref[layer]).astype(BF)
        total = bias_columns(spread, layer + 1)
        for a in range(3):
            pick = onehot(iota((144, KDIM), 0) == (3 * a + bk) * CH + (ck & 15))
            total = jnp.where(delta == a, 0.5 * dot(base, pick), total)
        out_ref[...] = total.astype(BF)
    last = jnp.broadcast_to(last_ref[...], (24, 144))
    delta = (iota((24, 160), 1) >> 4) - (iota((24, 160), 0) & 7)
    tap = iota((24, 160), 0) >> 3
    col = iota((144, 160), 1) & 15
    total = jnp.zeros((24, 160), F32)
    for b in range(3):
        for a in range(3):
            line = dot(last, onehot(iota((144, 160), 0) == (3 * a + b) * CH + col))
            total = jnp.where((delta == a) & (tap == b), line, total)
    w4_ref[...] = total.astype(BF)


def stack_kernel(recv_ref, w1_ref, pos_ref, out_ref, left_ref, right_ref):
    cells = []
    for s in range(OWNERS):
        extra = recv_ref[s, SLOTS:PAY, 0:SLOTS].astype(F32)
        cells.append((extra[0:1] - 1.0) * 32.0 + extra[1:2])
    cell = jnp.concatenate(cells, axis=1).astype(jnp.int32)
    total = OWNERS * SLOTS
    rows = recv_ref[:, 0:SLOTS, :].reshape(total, TS)
    lefts, rights = [], []
    step = 4
    for c in range(0, CL, step):
        hit = jnp.where(iota((step * MB, total), 0) + c * MB == cell, 1.0, 0.0)
        fold = jnp.maximum(jnp.sum(hit, axis=1, keepdims=True), 1.0)
        part = dot(hit.astype(BF), rows) / fold
        for k in range(step):
            piece = part[k * MB : (k + 1) * MB]
            out_ref[c + k] = piece.astype(BF)
            lefts.append(piece[:, 0:HALO])
            rights.append(piece[:, TS - HALO :])
    left_ref[...] = jnp.concatenate(lefts, axis=1).astype(BF)
    right_ref[...] = jnp.concatenate(rights, axis=1).astype(BF)


def transposed(blocks):
    group = iota(blocks[0].shape, 1) >> 4
    blocks = list(blocks)
    for bit in (1, 2, 4):
        keep = (group & bit) == 0
        for i in range(8):
            if i & bit == 0:
                a, b = blocks[i], blocks[i | bit]
                blocks[i] = jnp.where(keep, a, pltpu.roll(b, 16 * bit, 1))
                blocks[i | bit] = jnp.where(keep, pltpu.roll(a, TILE - 16 * bit, 1), b)
    return blocks


def swap_kernel(stack_ref, low_ref, high_ref, out_ref, first_ref, last_ref):
    side = jnp.concatenate([low_ref[...].astype(F32), high_ref[...].astype(F32)], axis=1)
    owner = (iota((MB, TILE), 1) >> 3) & 7
    rows = TS + TILE
    row = iota((rows, 1), 0)
    tau = row + HALO
    tau = jnp.where(row >= TS, row & 7, tau)
    tau = jnp.where(row >= TS + TILE // 2, (row & 7) + TS + HALO, tau)
    col = iota((1, 3 * TILE), 1)
    order = onehot(tau == TILES * (col & 15) + jnp.minimum(col >> 4, TILES - 1))
    full = []
    for c in range(CL):
        full.append(jnp.concatenate([stack_ref[c], jnp.where(owner == c, side, 0.0).astype(BF)], axis=1))
    mixed = dot(jnp.concatenate(full, axis=0), order)
    for half in range(2):
        blocks = [mixed[c * MB : (c + 1) * MB, half * TILE : (half + 1) * TILE] for c in range(CL)]
        for k, tile in enumerate(transposed(blocks)):
            k = 8 * half + k
            out_ref[:, k * TILE : (k + 1) * TILE] = tile.astype(BF)
    lane = iota((MB, TILE), 1) >> 4
    tile = jnp.zeros((MB, TILE), F32)
    for c in range(CL):
        tile = jnp.where(lane == c, mixed[c * MB : (c + 1) * MB, 2 * TILE :], tile)
    out_ref[:, 16 * TILE :] = tile.astype(BF)
    first_ref[...] = out_ref[0:HALO, :]
    last_ref[...] = out_ref[MB - HALO : MB, :]


def gelu_half(h):
    c0 = 2.0 * 0.7978845608028654
    c1 = 8.0 * 0.7978845608028654 * 0.044715
    return h + h * jnp.tanh(h * (c0 + c1 * (h * h)))


def turned(block, shift):
    return pltpu.roll(block, shift % TILE, 1)


def conv_kernel(pos_ref, core_ref, low_ref, high_ref, stack_ref, w1_ref, w2_ref, w3_ref, w4_ref, out_ref,
                x_ref, h1_ref, h2_ref, h3_ref, p_ref, mask_ref):
    mid = pos_ref[0]
    tm = pos_ref[1]
    lane = iota((CH, WIDE), 1)
    t = TILES * ((lane & 127) & 15) + (lane >> 7) - HALO + tm * TS
    keep = jnp.where((t >= 0) & (t < 4 * TS), 1.0, 0.0)
    mask_ref[0] = keep.astype(BF)
    mask_ref[1] = (keep * jnp.where(mid > 0, 1.0, 0.0)).astype(BF)
    mask_ref[2] = (keep * jnp.where(mid < 7, 1.0, 0.0)).astype(BF)

    def at(k):
        return slice((LEAD + k) * TILE, (LEAD + k + 1) * TILE)

    image = jnp.concatenate([low_ref[...].astype(F32), core_ref[...].astype(F32), high_ref[...].astype(F32)], axis=0)
    x_ref[:, TILE : TILE + LANES] = image.astype(BF)
    x_ref[:, 0:TILE] = pltpu.roll(image[:, 16 * TILE :], 1, 1).astype(BF)
    for k in range(2):
        x_ref[:, (18 + k) * TILE : (19 + k) * TILE] = pltpu.roll(image[:, k * TILE : (k + 1) * TILE], TILE - 1, 1).astype(BF)
    ones = jnp.ones((KDIM - TAPS, CHUNK), BF)
    chunks = [(k * CHUNK, min(CHUNK, LANES - k * CHUNK)) for k in range(NCHUNK)]
    h1_ref[R1 * CH :, :] = jnp.zeros((2 * CH, EXT), BF)
    h1_ref[:, (LEAD + 19) * TILE :] = jnp.zeros((80 * CH, 3 * TILE), BF)
    h2_ref[:, (LEAD + 21) * TILE :] = jnp.zeros((R2 * CH, TILE), BF)

    def finish(acc, row, base, wide, into_ref, slot, lead):
        which = 1 if row < 0 else (2 if row >= MB else 0)
        g = gelu_half(acc).astype(BF) * mask_ref[which, :, base : base + wide]
        into_ref[slot * CH : (slot + 1) * CH, base + lead * TILE : base + lead * TILE + wide] = g

    def layer1(base, wide):
        x = [x_ref[:, base + b * TILE : base + b * TILE + wide] for b in range(3)]
        x = jnp.concatenate(x + [ones[:, :wide]], axis=0)
        for s0 in range(0, R1, 13):
            acc = dot(w1_ref[s0 * CH : (s0 + 13) * CH, :], x)
            for j in range(13):
                finish(acc[j * CH : (j + 1) * CH], ORDER1[s0 + j] - 7, base, wide, h1_ref, s0 + j, LEAD)

    def window(ref, s0, base, wide, d):
        taps = []
        for b in range(3):
            lane = base + (LEAD + (b - 1) * d) * TILE
            taps.append(ref[s0 * CH : (s0 + 5) * CH, lane : lane + wide])
        return jnp.concatenate(taps + [ones[:, :wide]], axis=0)

    def layer2(base, wide):
        for s0 in range(0, R1 - 2, GROUP):
            acc = dot(w2_ref[...], window(h1_ref, s0, base, wide, 2))
            for j in range(GROUP):
                if s0 + j < R1 and ORDER1[s0 + j] < R2:
                    q = ORDER1[s0 + j]
                    finish(acc[j * CH : (j + 1) * CH], q - 5, base, wide, h2_ref, SLOT2[q], LEAD)

    def layer3(base, wide):
        for s0 in range(0, R2 - 2, GROUP):
            acc = dot(w3_ref[...], window(h2_ref, s0, base, wide, 4))
            for j in range(GROUP):
                if ORDER2[s0 + j] < R3:
                    q = ORDER2[s0 + j]
                    finish(acc[j * CH : (j + 1) * CH], q - 1, base, wide, h3_ref, q, 0)

    def layer4(base, wide):
        for q in range(0, MB, 8):
            acc = dot(w4_ref[...], h3_ref[q * CH : (q + 10) * CH, base : base + wide])
            for b in range(3):
                p_ref[b, q : q + 8, base + TILE : base + TILE + wide] = acc[8 * b : 8 * b + 8]

    def carry(ref, rows, width):
        for k in range(width):
            ref[:rows, at(TILES + k)] = turned(ref[:rows, at(k)], -1)
            ref[:rows, at(-1 - k)] = turned(ref[:rows, at(TILES - 1 - k)], 1)

    for n in range(NCHUNK):
        layer1(*chunks[n])
    carry(h1_ref, R1 * CH, 2)
    for n in (1, 2, 3, 4, 5, 6, 7, 8, 0):
        layer2(*chunks[n])
    carry(h2_ref, R2 * CH, 4)
    for n in (3, 4, 5, 6, 7, 8, 0, 1, 2):
        layer3(*chunks[n])
        layer4(*chunks[n])
    p_ref[0, :, 0:TILE] = pltpu.roll(p_ref[0, :, TILES * TILE : (TILES + 1) * TILE], 1, 1)
    p_ref[2, :, (TILES + 1) * TILE : (TILES + 2) * TILE] = pltpu.roll(p_ref[2, :, TILE : 2 * TILE], TILE - 1, 1)
    tiles = [
        p_ref[0, :, k * TILE : (k + 1) * TILE]
        + p_ref[1, :, (k + 1) * TILE : (k + 2) * TILE]
        + p_ref[2, :, (k + 2) * TILE : (k + 3) * TILE]
        for k in range(TILES)
    ]
    col = iota((3 * TILE, 1), 0)
    tau = jnp.where(col < SEG, TILES * (col & 15) + (col >> 4), -1)
    order = onehot(tau == iota((1, TS), 1) + HALO)
    firsts, seconds = transposed(tiles[0:8]), transposed(tiles[8:16])
    for c in range(CL):
        third = pltpu.roll(tiles[16], TILE - 16 * c, 1) if c else tiles[16]
        noise = jnp.concatenate([firsts[c], seconds[c], third], axis=1)
        top = noise.astype(BF)
        rest = (noise - top.astype(F32)).astype(BF)
        both = dot(jnp.concatenate([top, rest], axis=0), order)
        out_ref[c] = stack_ref[c].astype(F32) - (both[0:MB] + both[MB:])


def call(kernel, outs, scratch=(), smem=0, n=0, loose=0, name=None):
    specs = [pl.BlockSpec(memory_space=pltpu.SMEM) for _ in range(smem)]
    specs += [pl.BlockSpec(memory_space=pltpu.VMEM) for _ in range(n)]
    specs += [pl.BlockSpec(memory_space=pl.ANY) for _ in range(loose)]
    return pl.pallas_call(
        kernel,
        out_shape=outs,
        in_specs=specs,
        out_specs=jax.tree.map(lambda _: pl.BlockSpec(memory_space=pltpu.VMEM), outs),
        scratch_shapes=list(scratch),
        compiler_params=pltpu.CompilerParams(vmem_limit_bytes=60000 * 1024),
        name=name,
    )


def shape(*dims, dtype=BF):
    return jax.ShapeDtypeStruct(dims, dtype)


def near(x):
    return pltpu.with_memory_space_constraint(x, pltpu.VMEM)


def build_send(dest, cell, traces):
    return call(send_kernel, (shape(OWNERS, PAY, TS), shape(8, 128, dtype=F32)), n=3, name="send")(dest, cell, traces)


def build_weights(w_first, w_mid, w_last, bias, token):
    outs = (shape(R1 * CH, KDIM), shape(GROUP * CH, KDIM), shape(GROUP * CH, KDIM), shape(24, 160))
    return call(weights_kernel, outs, n=5, name="weights")(w_first, w_mid, w_last, bias, token)


def build_stack(recv, w1, pos):
    outs = (shape(CL, MB, TS), shape(MB, MB), shape(MB, MB))
    return call(stack_kernel, outs, n=1, loose=2, name="stack")(near(recv), w1, pos)


def reorder(stack, low, high):
    outs = (shape(MB, LANES), shape(HALO, LANES), shape(HALO, LANES))
    return call(swap_kernel, outs, n=3, name="reorder")(stack, near(low), near(high))


def convolve(pos, core, low, high, stack, weights):
    scratch = [
        pltpu.VMEM((80, 20 * TILE), BF),
        pltpu.VMEM((80 * CH, EXT), BF),
        pltpu.VMEM((R2 * CH, EXT), BF),
        pltpu.VMEM((R3 * CH, WIDE), BF),
        pltpu.VMEM((3, MB, 20 * TILE), F32),
        pltpu.VMEM((3, CH, WIDE), BF),
    ]
    return call(conv_kernel, shape(CL, MB, TS, dtype=F32), scratch, smem=1, n=8, name="conv")(
        pos, core, near(low), near(high), stack, *weights
    )


def neighbours(low_edge, high_edge, axis):
    count = lax.axis_size(axis)
    up = [(i, i + 1) for i in range(count - 1)]
    down = [(b, a) for a, b in up]
    return lax.ppermute(high_edge, axis, up), lax.ppermute(low_edge, axis, down)


def shards(traces, dest, cell, w_first, w_mid, w_last, bias):
    send, token = build_send(dest.reshape(1, COUNT), cell.reshape(1, COUNT), traces)
    recv = lax.all_to_all(send, ("offset", "mid"), split_axis=0, concat_axis=0, tiled=True)
    weights = build_weights(w_first, w_mid, w_last, bias, token)
    pos = jnp.stack([lax.axis_index("mid"), lax.axis_index("tm")]).astype(jnp.int32)
    stack, left, right = build_stack(recv, weights[0], pos)
    low, high = neighbours(left, right, "tm")
    core, first, last = reorder(stack, low, high)
    below, above = neighbours(first, last, "mid")
    return convolve(pos, core, below, above, stack, weights)


def solution(mesh):
    rows = P(("offset", "mid"), "tm")
    column = P(("offset", "mid"), None)
    placed = (rows, column, column, P(), P(), P(), P())
    return jax.shard_map(
        shards, mesh=mesh, in_specs=placed, out_specs=P("offset", "mid", "tm"), check_vma=False
    )
```

```python
import functools

import jax
import jax.numpy as jnp
from jax import lax
from jax.experimental import pallas as pl
from jax.experimental.pallas import tpu as pltpu
from jax.sharding import PartitionSpec as P

BF = jnp.bfloat16
F32 = jnp.float32
OWNERS = 32
SLOTS = 64
COUNT = 1024
TS = 256
CL = 8
MB = 64
HALO = 8
SEG = TS + 2 * HALO
LANES = CL * SEG
TILE = 128
TILES = 17
CHUNK = 2 * TILE
NCHUNK = 9
WIDE = CHUNK * NCHUNK
LEAD = 4
EXT = (LEAD + 22) * TILE
CH = 16
R1, R2, R3 = 78, 74, 66
TAPS = 240
KDIM = 256
GROUP = 3
EXTRA = 8
PAY = SLOTS + EXTRA


def slots_of(rows, groups):
    return [r for g in range(groups) for r in range(g, rows, groups)]


ORDER1 = slots_of(R1, 2)
ORDER2 = slots_of(R2, 4)
SLOT2 = {r: s for s, r in enumerate(ORDER2)}


def iota(shape, dim):
    return lax.broadcasted_iota(jnp.int32, shape, dim)


def onehot(mask):
    return jnp.where(mask, 1.0, 0.0).astype(BF)


def dot(a, b):
    return jnp.dot(a, b, preferred_element_type=F32)


def dot_t(a, b):
    return lax.dot_general(a, b, (((1,), (1,)), ((), ())), preferred_element_type=F32)


def send_kernel(dest_ref, cell_ref, traces_ref, out_hbm, token_ref, out_ref, sems):
    dest = dest_ref[...]
    cell = cell_ref[...]
    width = 256
    blocks = COUNT // width
    owner = iota((OWNERS, width), 0)
    hots = [owner == dest[:, n * width : (n + 1) * width] for n in range(blocks)]
    upper = onehot(iota((width, width), 0) < iota((width, width), 1))
    before = dot(jnp.concatenate([onehot(hot) for hot in hots], axis=0), upper)
    ranks = []
    offset = jnp.zeros((OWNERS, 1), F32)
    for n, hot in enumerate(hots):
        part = before[n * OWNERS : (n + 1) * OWNERS]
        ranks.append(jnp.sum(jnp.where(hot, part + offset, 0.0), axis=0, keepdims=True))
        offset = offset + jnp.sum(jnp.where(hot, 1.0, 0.0), axis=1, keepdims=True)
    rank = jnp.concatenate(ranks, axis=1)
    place = dest * SLOTS + rank.astype(jnp.int32)
    high = (cell >> 5) + 1
    low = cell & 31
    row = iota((16, COUNT), 0)
    meta = jnp.where(row == 0, high, jnp.where(row == 1, low, 0)).astype(F32).astype(BF)
    traces = traces_ref[...]
    blank = jnp.zeros((EXTRA, TS - SLOTS), F32)
    step = 8
    copies = []
    for o in range(0, OWNERS, step):
        slot = iota((step * SLOTS, COUNT), 0) + o * SLOTS
        placing = onehot(slot == place)
        rows = dot(placing, traces).astype(BF)
        extra = dot_t(meta, placing)
        for k in range(step):
            out_ref[o + k, 0:SLOTS, :] = rows[k * SLOTS : (k + 1) * SLOTS]
            part = extra[0:EXTRA, k * SLOTS : (k + 1) * SLOTS]
            out_ref[o + k, SLOTS:PAY, :] = jnp.concatenate([part, blank], axis=1).astype(BF)
        copy = pltpu.make_async_copy(out_ref.at[o : o + step], out_hbm.at[o : o + step], sems.at[o // step])
        copy.start()
        copies.append(copy)
    token_ref[...] = jnp.zeros(token_ref.shape, F32) + rank[:, 0:128]
    for copy in copies:
        copy.wait()


def weights_kernel(first_ref, mid_ref, last_ref, bias_ref, token_ref, w1_ref, w2_ref, w3_ref, w4_ref):
    bias = 0.5 * bias_ref[...]
    parts = []
    for _ in range(3):
        part = bias.astype(BF)
        parts.append(part)
        bias = bias - part.astype(F32)

    def bias_columns(spread, layer):
        row = iota((16, CH), 0)
        lines = jnp.zeros((16, CH), F32)
        for e in range(3):
            lines = jnp.where(row == e, parts[e][layer : layer + 1].astype(F32), lines)
        spreaded = dot_t(spread, lines.astype(BF)).astype(BF)
        return dot(spreaded, onehot(iota((16, KDIM), 1) == iota((16, KDIM), 0) + TAPS))

    step = 6 * CH
    first = first_ref[...]
    c = iota((step, KDIM), 1)
    b = jnp.where(c >= 80, 1, 0) + jnp.where(c >= 160, 1, 0)
    m = jnp.where(c < TAPS, c - 80 * b, -100)
    ck = iota((9, KDIM), 1)
    bk = jnp.where(ck >= 80, 1, 0) + jnp.where(ck >= 160, 1, 0)
    spread = onehot((iota((step, CH), 0) & (CH - 1)) == iota((step, CH), 1))
    base = dot(spread, first).astype(BF)
    picked = [0.5 * dot(base, onehot(iota((9, KDIM), 0) == 3 * a + bk)) for a in range(3)]
    other = bias_columns(spread, 0)
    for n in range(R1 * CH // step):
        r = (iota((step, KDIM), 0) >> 4) + 6 * n
        r = jnp.where(r < R1 // 2, 2 * r, 2 * r - (R1 - 1))
        total = other
        for a in range(3):
            total = jnp.where(m - r == a, picked[a], total)
        w1_ref[n * step : (n + 1) * step, :] = total.astype(BF)
    rows = GROUP * CH
    spread = onehot((iota((rows, CH), 0) & (CH - 1)) == iota((rows, CH), 1))
    c = iota((rows, KDIM), 1)
    b = jnp.where(c >= 80, 1, 0) + jnp.where(c >= 160, 1, 0)
    delta = jnp.where(c < TAPS, ((c - 80 * b) >> 4) - (iota((rows, KDIM), 0) >> 4), -100)
    ck = iota((144, KDIM), 1)
    bk = jnp.where(ck >= 80, 1, 0) + jnp.where(ck >= 160, 1, 0)
    for layer, out_ref in ((0, w2_ref), (1, w3_ref)):
        base = dot(spread, mid_ref[layer]).astype(BF)
        total = bias_columns(spread, layer + 1)
        for a in range(3):
            pick = onehot(iota((144, KDIM), 0) == (3 * a + bk) * CH + (ck & 15))
            total = jnp.where(delta == a, 0.5 * dot(base, pick), total)
        out_ref[...] = total.astype(BF)
    last = jnp.broadcast_to(last_ref[...], (24, 144))
    delta = (iota((24, 160), 1) >> 4) - (iota((24, 160), 0) & 7)
    tap = iota((24, 160), 0) >> 3
    col = iota((144, 160), 1) & 15
    total = jnp.zeros((24, 160), F32)
    for b in range(3):
        for a in range(3):
            line = dot(last, onehot(iota((144, 160), 0) == (3 * a + b) * CH + col))
            total = jnp.where((delta == a) & (tap == b), line, total)
    w4_ref[...] = total.astype(BF)


def stack_kernel(recv_ref, w1_ref, pos_ref, out_ref, left_ref, right_ref):
    cells = []
    for s in range(OWNERS):
        extra = recv_ref[s, SLOTS:PAY, 0:SLOTS].astype(F32)
        cells.append((extra[0:1] - 1.0) * 32.0 + extra[1:2])
    cell = jnp.concatenate(cells, axis=1).astype(jnp.int32)
    total = OWNERS * SLOTS
    rows = recv_ref[:, 0:SLOTS, :].reshape(total, TS)
    lefts, rights = [], []
    step = 4
    for c in range(0, CL, step):
        hit = jnp.where(iota((step * MB, total), 0) + c * MB == cell, 1.0, 0.0)
        fold = jnp.maximum(jnp.sum(hit, axis=1, keepdims=True), 1.0)
        part = dot(hit.astype(BF), rows) / fold
        for k in range(step):
            piece = part[k * MB : (k + 1) * MB]
            out_ref[c + k] = piece.astype(BF)
            lefts.append(piece[:, 0:HALO])
            rights.append(piece[:, TS - HALO :])
    left_ref[...] = jnp.concatenate(lefts, axis=1).astype(BF)
    right_ref[...] = jnp.concatenate(rights, axis=1).astype(BF)


def transposed(blocks):
    group = iota(blocks[0].shape, 1) >> 4
    blocks = list(blocks)
    for bit in (1, 2, 4):
        keep = (group & bit) == 0
        for i in range(8):
            if i & bit == 0:
                a, b = blocks[i], blocks[i | bit]
                blocks[i] = jnp.where(keep, a, pltpu.roll(b, 16 * bit, 1))
                blocks[i | bit] = jnp.where(keep, pltpu.roll(a, TILE - 16 * bit, 1), b)
    return blocks


def swap_kernel(stack_ref, low_ref, high_ref, out_ref, first_ref, last_ref):
    side = jnp.concatenate([low_ref[...].astype(F32), high_ref[...].astype(F32)], axis=1)
    owner = (iota((MB, TILE), 1) >> 3) & 7
    rows = TS + TILE
    row = iota((rows, 1), 0)
    tau = row + HALO
    tau = jnp.where(row >= TS, row & 7, tau)
    tau = jnp.where(row >= TS + TILE // 2, (row & 7) + TS + HALO, tau)
    col = iota((1, 3 * TILE), 1)
    order = onehot(tau == TILES * (col & 15) + jnp.minimum(col >> 4, TILES - 1))
    full = []
    for c in range(CL):
        full.append(jnp.concatenate([stack_ref[c], jnp.where(owner == c, side, 0.0).astype(BF)], axis=1))
    mixed = dot(jnp.concatenate(full, axis=0), order)
    for half in range(2):
        blocks = [mixed[c * MB : (c + 1) * MB, half * TILE : (half + 1) * TILE] for c in range(CL)]
        for k, tile in enumerate(transposed(blocks)):
            k = 8 * half + k
            out_ref[:, k * TILE : (k + 1) * TILE] = tile.astype(BF)
    lane = iota((MB, TILE), 1) >> 4
    tile = jnp.zeros((MB, TILE), F32)
    for c in range(CL):
        tile = jnp.where(lane == c, mixed[c * MB : (c + 1) * MB, 2 * TILE :], tile)
    out_ref[:, 16 * TILE :] = tile.astype(BF)
    first_ref[...] = out_ref[0:HALO, :]
    last_ref[...] = out_ref[MB - HALO : MB, :]


def gelu_half(h):
    c0 = 2.0 * 0.7978845608028654
    c1 = 8.0 * 0.7978845608028654 * 0.044715
    return h + h * jnp.tanh(h * (c0 + c1 * (h * h)))


def turned(block, shift):
    return pltpu.roll(block, shift % TILE, 1)


def conv_kernel(pos_ref, core_ref, low_ref, high_ref, stack_ref, w1_ref, w2_ref, w3_ref, w4_ref, out_ref,
                x_ref, h1_ref, h2_ref, h3_ref, p_ref, mask_ref):
    mid = pos_ref[0]
    tm = pos_ref[1]
    lane = iota((CH, WIDE), 1)
    t = TILES * ((lane & 127) & 15) + (lane >> 7) - HALO + tm * TS
    keep = jnp.where((t >= 0) & (t < 4 * TS), 1.0, 0.0)
    mask_ref[0] = keep.astype(BF)
    mask_ref[1] = (keep * jnp.where(mid > 0, 1.0, 0.0)).astype(BF)
    mask_ref[2] = (keep * jnp.where(mid < 7, 1.0, 0.0)).astype(BF)

    def at(k):
        return slice((LEAD + k) * TILE, (LEAD + k + 1) * TILE)

    image = jnp.concatenate([low_ref[...].astype(F32), core_ref[...].astype(F32), high_ref[...].astype(F32)], axis=0)
    x_ref[:, TILE : TILE + LANES] = image.astype(BF)
    x_ref[:, 0:TILE] = pltpu.roll(image[:, 16 * TILE :], 1, 1).astype(BF)
    for k in range(2):
        x_ref[:, (18 + k) * TILE : (19 + k) * TILE] = pltpu.roll(image[:, k * TILE : (k + 1) * TILE], TILE - 1, 1).astype(BF)
    ones = jnp.ones((KDIM - TAPS, CHUNK), BF)
    chunks = [(k * CHUNK, min(CHUNK, LANES - k * CHUNK)) for k in range(NCHUNK)]
    h1_ref[R1 * CH :, :] = jnp.zeros((2 * CH, EXT), BF)
    h1_ref[:, (LEAD + 19) * TILE :] = jnp.zeros((80 * CH, 3 * TILE), BF)
    h2_ref[:, (LEAD + 21) * TILE :] = jnp.zeros((R2 * CH, TILE), BF)

    def finish(acc, row, base, wide, into_ref, slot, lead):
        which = 1 if row < 0 else (2 if row >= MB else 0)
        g = gelu_half(acc).astype(BF) * mask_ref[which, :, base : base + wide]
        into_ref[slot * CH : (slot + 1) * CH, base + lead * TILE : base + lead * TILE + wide] = g

    def layer1(base, wide):
        x = [x_ref[:, base + b * TILE : base + b * TILE + wide] for b in range(3)]
        x = jnp.concatenate(x + [ones[:, :wide]], axis=0)
        for s0 in range(0, R1, 13):
            acc = dot(w1_ref[s0 * CH : (s0 + 13) * CH, :], x)
            for j in range(13):
                finish(acc[j * CH : (j + 1) * CH], ORDER1[s0 + j] - 7, base, wide, h1_ref, s0 + j, LEAD)

    def window(ref, s0, base, wide, d):
        taps = []
        for b in range(3):
            lane = base + (LEAD + (b - 1) * d) * TILE
            taps.append(ref[s0 * CH : (s0 + 5) * CH, lane : lane + wide])
        return jnp.concatenate(taps + [ones[:, :wide]], axis=0)

    def layer2(base, wide):
        for s0 in range(0, R1 - 2, GROUP):
            acc = dot(w2_ref[...], window(h1_ref, s0, base, wide, 2))
            for j in range(GROUP):
                if s0 + j < R1 and ORDER1[s0 + j] < R2:
                    q = ORDER1[s0 + j]
                    finish(acc[j * CH : (j + 1) * CH], q - 5, base, wide, h2_ref, SLOT2[q], LEAD)

    def layer3(base, wide):
        for s0 in range(0, R2 - 2, GROUP):
            acc = dot(w3_ref[...], window(h2_ref, s0, base, wide, 4))
            for j in range(GROUP):
                if ORDER2[s0 + j] < R3:
                    q = ORDER2[s0 + j]
                    finish(acc[j * CH : (j + 1) * CH], q - 1, base, wide, h3_ref, q, 0)

    def layer4(base, wide):
        for q in range(0, MB, 8):
            acc = dot(w4_ref[...], h3_ref[q * CH : (q + 10) * CH, base : base + wide])
            for b in range(3):
                p_ref[b, q : q + 8, base + TILE : base + TILE + wide] = acc[8 * b : 8 * b + 8]

    def carry(ref, rows, width):
        for k in range(width):
            ref[:rows, at(TILES + k)] = turned(ref[:rows, at(k)], -1)
            ref[:rows, at(-1 - k)] = turned(ref[:rows, at(TILES - 1 - k)], 1)

    for n in range(NCHUNK):
        layer1(*chunks[n])
    carry(h1_ref, R1 * CH, 2)
    for n in (1, 2, 3, 4, 5, 6, 7, 8, 0):
        layer2(*chunks[n])
    carry(h2_ref, R2 * CH, 4)
    for n in (3, 4, 5, 6, 7, 8, 0, 1, 2):
        layer3(*chunks[n])
        layer4(*chunks[n])
    p_ref[0, :, 0:TILE] = pltpu.roll(p_ref[0, :, TILES * TILE : (TILES + 1) * TILE], 1, 1)
    p_ref[2, :, (TILES + 1) * TILE : (TILES + 2) * TILE] = pltpu.roll(p_ref[2, :, TILE : 2 * TILE], TILE - 1, 1)
    tiles = [
        p_ref[0, :, k * TILE : (k + 1) * TILE]
        + p_ref[1, :, (k + 1) * TILE : (k + 2) * TILE]
        + p_ref[2, :, (k + 2) * TILE : (k + 3) * TILE]
        for k in range(TILES)
    ]
    col = iota((3 * TILE, 1), 0)
    tau = jnp.where(col < SEG, TILES * (col & 15) + (col >> 4), -1)
    order = onehot(tau == iota((1, TS), 1) + HALO)
    firsts, seconds = transposed(tiles[0:8]), transposed(tiles[8:16])
    for c in range(CL):
        third = pltpu.roll(tiles[16], TILE - 16 * c, 1) if c else tiles[16]
        noise = jnp.concatenate([firsts[c], seconds[c], third], axis=1)
        top = noise.astype(BF)
        rest = (noise - top.astype(F32)).astype(BF)
        both = dot(jnp.concatenate([top, rest], axis=0), order)
        out_ref[c] = stack_ref[c].astype(F32) - (both[0:MB] + both[MB:])


def call(kernel, outs, scratch=(), smem=0, n=0, loose=0, name=None, limit=20, where=None):
    specs = [pl.BlockSpec(memory_space=pltpu.SMEM) for _ in range(smem)]
    specs += [pl.BlockSpec(memory_space=pltpu.VMEM) for _ in range(n)]
    specs += [pl.BlockSpec(memory_space=pl.ANY) for _ in range(loose)]
    number = len(outs) if isinstance(outs, tuple) else 1
    out_specs = tuple(pl.BlockSpec(memory_space=space) for space in where or (pltpu.VMEM,) * number)
    return pl.pallas_call(
        kernel,
        out_shape=outs,
        in_specs=specs,
        out_specs=out_specs if isinstance(outs, tuple) else out_specs[0],
        scratch_shapes=list(scratch),
        compiler_params=pltpu.CompilerParams(vmem_limit_bytes=limit * 2**20),
        name=name,
    )


def shape(*dims, dtype=BF):
    return pltpu.VMEM(dims, dtype)


def near(x):
    return pltpu.with_memory_space_constraint(x, pltpu.VMEM)


def build_send(dest, cell, traces):
    outs = (jax.ShapeDtypeStruct((OWNERS, PAY, TS), BF), jax.ShapeDtypeStruct((8, 128), F32))
    scratch = [pltpu.VMEM((OWNERS, PAY, TS), BF), pltpu.SemaphoreType.DMA((4,))]
    return call(send_kernel, outs, scratch, n=3, name="send", where=(pl.ANY, pltpu.VMEM))(dest, cell, traces)


def build_weights(w_first, w_mid, w_last, bias, token):
    outs = (shape(R1 * CH, KDIM), shape(GROUP * CH, KDIM), shape(GROUP * CH, KDIM), shape(24, 160))
    return call(weights_kernel, outs, n=5, name="weights")(w_first, w_mid, w_last, bias, token)


def build_stack(recv, w1, pos):
    outs = (shape(CL, MB, TS), shape(MB, MB), shape(MB, MB))
    return call(stack_kernel, outs, n=1, loose=2, name="stack")(near(recv), w1, pos)


def reorder(stack, low, high):
    outs = (shape(MB, LANES), shape(HALO, LANES), shape(HALO, LANES))
    return call(swap_kernel, outs, n=3, name="reorder")(near(stack), near(low), near(high))


def convolve(pos, core, low, high, stack, weights):
    scratch = [
        pltpu.VMEM((80, 20 * TILE), BF),
        pltpu.VMEM((80 * CH, EXT), BF),
        pltpu.VMEM((R2 * CH, EXT), BF),
        pltpu.VMEM((R3 * CH, WIDE), BF),
        pltpu.VMEM((3, MB, 20 * TILE), F32),
        pltpu.VMEM((3, CH, WIDE), BF),
    ]
    return call(conv_kernel, jax.ShapeDtypeStruct((CL, MB, TS), F32), scratch, smem=1, n=8, name="conv", limit=40)(
        pos, near(core), near(low), near(high), near(stack), *[near(w) for w in weights]
    )


def neighbours(low_edge, high_edge, axis):
    count = lax.axis_size(axis)
    up = [(i, i + 1) for i in range(count - 1)]
    down = [(b, a) for a, b in up]
    return lax.ppermute(high_edge, axis, up), lax.ppermute(low_edge, axis, down)


def shards(traces, dest, cell, w_first, w_mid, w_last, bias):
    send, token = build_send(dest.reshape(1, COUNT), cell.reshape(1, COUNT), traces)
    recv = lax.all_to_all(send, ("offset", "mid"), split_axis=0, concat_axis=0, tiled=True)
    weights = build_weights(w_first, w_mid, w_last, bias, token)
    pos = jnp.stack([lax.axis_index("mid"), lax.axis_index("tm")]).astype(jnp.int32)
    stack, left, right = build_stack(recv, weights[0], pos)
    low, high = neighbours(left, right, "tm")
    core, first, last = reorder(stack, low, high)
    below, above = neighbours(first, last, "mid")
    return convolve(pos, core, below, above, stack, weights)


def solution(mesh):
    rows = P(("offset", "mid"), "tm")
    column = P(("offset", "mid"), None)
    placed = (rows, column, column, P(), P(), P(), P())
    return jax.shard_map(
        shards, mesh=mesh, in_specs=placed, out_specs=P("offset", "mid", "tm"), check_vma=False
    )
```

```python
import functools

import jax
import jax.numpy as jnp
from jax import lax
from jax.experimental import pallas as pl
from jax.experimental.pallas import tpu as pltpu
from jax.sharding import PartitionSpec as P

BF = jnp.bfloat16
F32 = jnp.float32
OWNERS = 32
SLOTS = 64
COUNT = 1024
TS = 256
CL = 8
MB = 64
HALO = 8
SEG = TS + 2 * HALO
LANES = CL * SEG
TILE = 128
TILES = 17
CHUNK = 2 * TILE
NCHUNK = 9
WIDE = CHUNK * NCHUNK
LEAD = 4
EXT = (LEAD + 22) * TILE
CH = 16
R1, R2, R3 = 78, 74, 66
TAPS = 240
KDIM = 256
GROUP = 3
EXTRA = 8
PAY = 2 * SLOTS + EXTRA


def slots_of(rows, groups):
    return [r for g in range(groups) for r in range(g, rows, groups)]


ORDER1 = slots_of(R1, 2)
ORDER2 = slots_of(R2, 4)
SLOT2 = {r: s for s, r in enumerate(ORDER2)}


def iota(shape, dim):
    return lax.broadcasted_iota(jnp.int32, shape, dim)


def onehot(mask):
    return jnp.where(mask, 1.0, 0.0).astype(BF)


def dot(a, b):
    return jnp.dot(a, b, preferred_element_type=F32)


def dot_t(a, b):
    return lax.dot_general(a, b, (((1,), (1,)), ((), ())), preferred_element_type=F32)


def send_kernel(dest_hbm, cell_hbm, traces_hbm, out_hbm, token_ref, out_ref, sems, dest_ref, cell_ref, traces_ref, ins):
    loads = [
        pltpu.make_async_copy(source, target, ins.at[n])
        for n, (source, target) in enumerate(((dest_hbm, dest_ref), (cell_hbm, cell_ref), (traces_hbm, traces_ref)))
    ]
    for load in loads:
        load.start()
    for load in loads[:2]:
        load.wait()
    dest = dest_ref[...]
    cell = cell_ref[...]
    width = 256
    blocks = COUNT // width
    owner = iota((OWNERS, width), 0)
    hots = [owner == dest[:, n * width : (n + 1) * width] for n in range(blocks)]
    upper = onehot(iota((width, width), 0) < iota((width, width), 1))
    before = dot(jnp.concatenate([onehot(hot) for hot in hots], axis=0), upper)
    ranks = []
    offset = jnp.zeros((OWNERS, 1), F32)
    for n, hot in enumerate(hots):
        part = before[n * OWNERS : (n + 1) * OWNERS]
        ranks.append(jnp.sum(jnp.where(hot, part + offset, 0.0), axis=0, keepdims=True))
        offset = offset + jnp.sum(jnp.where(hot, 1.0, 0.0), axis=1, keepdims=True)
    rank = jnp.concatenate(ranks, axis=1)
    place = dest * SLOTS + rank.astype(jnp.int32)
    high = (cell >> 5) + 1
    low = cell & 31
    row = iota((16, COUNT), 0)
    meta = jnp.where(row == 0, high, jnp.where(row == 1, low, 0)).astype(F32).astype(BF)
    loads[2].wait()
    traces = traces_ref[...]
    blank = jnp.zeros((EXTRA, TILE - SLOTS), F32)
    step = 8
    copies = []
    for o in range(0, OWNERS, step):
        slot = iota((step * SLOTS, COUNT), 0) + o * SLOTS
        placing = onehot(slot == place)
        rows = dot(placing, traces).astype(BF)
        extra = dot_t(meta, placing)
        for k in range(step):
            out_ref[o + k, 0:SLOTS, :] = rows[k * SLOTS : (k + 1) * SLOTS, 0:TILE]
            out_ref[o + k, SLOTS : 2 * SLOTS, :] = rows[k * SLOTS : (k + 1) * SLOTS, TILE:]
            part = extra[0:EXTRA, k * SLOTS : (k + 1) * SLOTS]
            out_ref[o + k, 2 * SLOTS : PAY, :] = jnp.concatenate([part, blank], axis=1).astype(BF)
        copy = pltpu.make_async_copy(out_ref.at[o : o + step], out_hbm.at[o : o + step], sems.at[o // step])
        copy.start()
        copies.append(copy)
    token_ref[...] = jnp.zeros(token_ref.shape, F32) + rank[:, 0:128]
    for copy in copies:
        copy.wait()


def weights_kernel(first_ref, mid_ref, last_ref, bias_ref, token_ref, w1_ref, w2_ref, w3_ref, w4_ref):
    bias = 0.5 * bias_ref[...]
    parts = []
    for _ in range(3):
        part = bias.astype(BF)
        parts.append(part)
        bias = bias - part.astype(F32)

    def bias_columns(spread, layer):
        row = iota((16, CH), 0)
        lines = jnp.zeros((16, CH), F32)
        for e in range(3):
            lines = jnp.where(row == e, parts[e][layer : layer + 1].astype(F32), lines)
        spreaded = dot_t(spread, lines.astype(BF)).astype(BF)
        return dot(spreaded, onehot(iota((16, KDIM), 1) == iota((16, KDIM), 0) + TAPS))

    step = 6 * CH
    first = first_ref[...]
    c = iota((step, KDIM), 1)
    b = jnp.where(c >= 80, 1, 0) + jnp.where(c >= 160, 1, 0)
    m = jnp.where(c < TAPS, c - 80 * b, -100)
    ck = iota((9, KDIM), 1)
    bk = jnp.where(ck >= 80, 1, 0) + jnp.where(ck >= 160, 1, 0)
    spread = onehot((iota((step, CH), 0) & (CH - 1)) == iota((step, CH), 1))
    base = dot(spread, first).astype(BF)
    picked = [0.5 * dot(base, onehot(iota((9, KDIM), 0) == 3 * a + bk)) for a in range(3)]
    other = bias_columns(spread, 0)
    for n in range(R1 * CH // step):
        r = (iota((step, KDIM), 0) >> 4) + 6 * n
        r = jnp.where(r < R1 // 2, 2 * r, 2 * r - (R1 - 1))
        total = other
        for a in range(3):
            total = jnp.where(m - r == a, picked[a], total)
        w1_ref[n * step : (n + 1) * step, :] = total.astype(BF)
    rows = GROUP * CH
    spread = onehot((iota((rows, CH), 0) & (CH - 1)) == iota((rows, CH), 1))
    c = iota((rows, KDIM), 1)
    b = jnp.where(c >= 80, 1, 0) + jnp.where(c >= 160, 1, 0)
    delta = jnp.where(c < TAPS, ((c - 80 * b) >> 4) - (iota((rows, KDIM), 0) >> 4), -100)
    ck = iota((144, KDIM), 1)
    bk = jnp.where(ck >= 80, 1, 0) + jnp.where(ck >= 160, 1, 0)
    for layer, out_ref in ((0, w2_ref), (1, w3_ref)):
        base = dot(spread, mid_ref[layer]).astype(BF)
        total = bias_columns(spread, layer + 1)
        for a in range(3):
            pick = onehot(iota((144, KDIM), 0) == (3 * a + bk) * CH + (ck & 15))
            total = jnp.where(delta == a, 0.5 * dot(base, pick), total)
        out_ref[...] = total.astype(BF)
    last = jnp.broadcast_to(last_ref[...], (24, 144))
    delta = (iota((24, 160), 1) >> 4) - (iota((24, 160), 0) & 7)
    tap = iota((24, 160), 0) >> 3
    col = iota((144, 160), 1) & 15
    total = jnp.zeros((24, 160), F32)
    for b in range(3):
        for a in range(3):
            line = dot(last, onehot(iota((144, 160), 0) == (3 * a + b) * CH + col))
            total = jnp.where((delta == a) & (tap == b), line, total)
    w4_ref[...] = total.astype(BF)


def stack_kernel(recv_ref, w1_ref, pos_ref, out_ref, left_ref, right_ref):
    cells = []
    for s in range(OWNERS):
        extra = recv_ref[s, 2 * SLOTS : PAY, 0:SLOTS].astype(F32)
        cells.append((extra[0:1] - 1.0) * 32.0 + extra[1:2])
    cell = jnp.concatenate(cells, axis=1).astype(jnp.int32)
    total = OWNERS * SLOTS
    rows = jnp.concatenate(
        [recv_ref[:, 0:SLOTS, :].reshape(total, TILE), recv_ref[:, SLOTS : 2 * SLOTS, :].reshape(total, TILE)], axis=1
    )
    lefts, rights = [], []
    step = 4
    for c in range(0, CL, step):
        hit = jnp.where(iota((step * MB, total), 0) + c * MB == cell, 1.0, 0.0)
        fold = jnp.maximum(jnp.sum(hit, axis=1, keepdims=True), 1.0)
        part = dot(hit.astype(BF), rows) / fold
        for k in range(step):
            piece = part[k * MB : (k + 1) * MB]
            out_ref[c + k] = piece.astype(BF)
            lefts.append(piece[:, 0:HALO])
            rights.append(piece[:, TS - HALO :])
    left_ref[...] = jnp.concatenate(lefts, axis=1).astype(BF)
    right_ref[...] = jnp.concatenate(rights, axis=1).astype(BF)


def transposed(blocks):
    group = iota(blocks[0].shape, 1) >> 4
    blocks = list(blocks)
    for bit in (1, 2, 4):
        keep = (group & bit) == 0
        for i in range(8):
            if i & bit == 0:
                a, b = blocks[i], blocks[i | bit]
                blocks[i] = jnp.where(keep, a, pltpu.roll(b, 16 * bit, 1))
                blocks[i | bit] = jnp.where(keep, pltpu.roll(a, TILE - 16 * bit, 1), b)
    return blocks


def swap_kernel(stack_ref, low_ref, high_ref, out_ref, first_ref, last_ref):
    side = jnp.concatenate([low_ref[...].astype(F32), high_ref[...].astype(F32)], axis=1)
    owner = (iota((MB, TILE), 1) >> 3) & 7
    rows = TS + TILE
    row = iota((rows, 1), 0)
    tau = row + HALO
    tau = jnp.where(row >= TS, row & 7, tau)
    tau = jnp.where(row >= TS + TILE // 2, (row & 7) + TS + HALO, tau)
    col = iota((1, 3 * TILE), 1)
    order = onehot(tau == TILES * (col & 15) + jnp.minimum(col >> 4, TILES - 1))
    full = []
    for c in range(CL):
        full.append(jnp.concatenate([stack_ref[c], jnp.where(owner == c, side, 0.0).astype(BF)], axis=1))
    mixed = dot(jnp.concatenate(full, axis=0), order)
    for half in range(2):
        blocks = [mixed[c * MB : (c + 1) * MB, half * TILE : (half + 1) * TILE] for c in range(CL)]
        for k, tile in enumerate(transposed(blocks)):
            k = 8 * half + k
            out_ref[:, k * TILE : (k + 1) * TILE] = tile.astype(BF)
    lane = iota((MB, TILE), 1) >> 4
    tile = jnp.zeros((MB, TILE), F32)
    for c in range(CL):
        tile = jnp.where(lane == c, mixed[c * MB : (c + 1) * MB, 2 * TILE :], tile)
    out_ref[:, 16 * TILE :] = tile.astype(BF)
    first_ref[...] = out_ref[0:HALO, :]
    last_ref[...] = out_ref[MB - HALO : MB, :]


def gelu_half(h):
    c0 = 2.0 * 0.7978845608028654
    c1 = 8.0 * 0.7978845608028654 * 0.044715
    return h + h * jnp.tanh(h * (c0 + c1 * (h * h)))


def turned(block, shift):
    return pltpu.roll(block, shift % TILE, 1)


def conv_kernel(pos_ref, core_ref, low_ref, high_ref, stack_ref, w1_ref, w2_ref, w3_ref, w4_ref, out_hbm,
                out_ref, sems, x_ref, h1_ref, h2_ref, h3_ref, p_ref, mask_ref):
    mid = pos_ref[0]
    tm = pos_ref[1]
    lane = iota((CH, WIDE), 1)
    t = TILES * ((lane & 127) & 15) + (lane >> 7) - HALO + tm * TS
    keep = jnp.where((t >= 0) & (t < 4 * TS), 1.0, 0.0)
    mask_ref[0] = keep.astype(BF)
    mask_ref[1] = (keep * jnp.where(mid > 0, 1.0, 0.0)).astype(BF)
    mask_ref[2] = (keep * jnp.where(mid < 7, 1.0, 0.0)).astype(BF)

    def at(k):
        return slice((LEAD + k) * TILE, (LEAD + k + 1) * TILE)

    image = jnp.concatenate([low_ref[...].astype(F32), core_ref[...].astype(F32), high_ref[...].astype(F32)], axis=0)
    x_ref[:, TILE : TILE + LANES] = image.astype(BF)
    x_ref[:, 0:TILE] = pltpu.roll(image[:, 16 * TILE :], 1, 1).astype(BF)
    for k in range(2):
        x_ref[:, (18 + k) * TILE : (19 + k) * TILE] = pltpu.roll(image[:, k * TILE : (k + 1) * TILE], TILE - 1, 1).astype(BF)
    ones = jnp.ones((KDIM - TAPS, CHUNK), BF)
    chunks = [(k * CHUNK, min(CHUNK, LANES - k * CHUNK)) for k in range(NCHUNK)]
    h1_ref[R1 * CH :, :] = jnp.zeros((2 * CH, EXT), BF)
    h1_ref[:, (LEAD + 19) * TILE :] = jnp.zeros((80 * CH, 3 * TILE), BF)
    h2_ref[:, (LEAD + 21) * TILE :] = jnp.zeros((R2 * CH, TILE), BF)

    def finish(acc, row, base, wide, into_ref, slot, lead):
        which = 1 if row < 0 else (2 if row >= MB else 0)
        g = gelu_half(acc).astype(BF) * mask_ref[which, :, base : base + wide]
        into_ref[slot * CH : (slot + 1) * CH, base + lead * TILE : base + lead * TILE + wide] = g

    def layer1(base, wide):
        x = [x_ref[:, base + b * TILE : base + b * TILE + wide] for b in range(3)]
        x = jnp.concatenate(x + [ones[:, :wide]], axis=0)
        for s0 in range(0, R1, 13):
            acc = dot(w1_ref[s0 * CH : (s0 + 13) * CH, :], x)
            for j in range(13):
                finish(acc[j * CH : (j + 1) * CH], ORDER1[s0 + j] - 7, base, wide, h1_ref, s0 + j, LEAD)

    def window(ref, s0, base, wide, d):
        taps = []
        for b in range(3):
            lane = base + (LEAD + (b - 1) * d) * TILE
            taps.append(ref[s0 * CH : (s0 + 5) * CH, lane : lane + wide])
        return jnp.concatenate(taps + [ones[:, :wide]], axis=0)

    def layer2(base, wide):
        for s0 in range(0, R1 - 2, GROUP):
            acc = dot(w2_ref[...], window(h1_ref, s0, base, wide, 2))
            for j in range(GROUP):
                if s0 + j < R1 and ORDER1[s0 + j] < R2:
                    q = ORDER1[s0 + j]
                    finish(acc[j * CH : (j + 1) * CH], q - 5, base, wide, h2_ref, SLOT2[q], LEAD)

    def layer3(base, wide):
        for s0 in range(0, R2 - 2, GROUP):
            acc = dot(w3_ref[...], window(h2_ref, s0, base, wide, 4))
            for j in range(GROUP):
                if ORDER2[s0 + j] < R3:
                    q = ORDER2[s0 + j]
                    finish(acc[j * CH : (j + 1) * CH], q - 1, base, wide, h3_ref, q, 0)

    def layer4(base, wide):
        for q in range(0, MB, 8):
            acc = dot(w4_ref[...], h3_ref[q * CH : (q + 10) * CH, base : base + wide])
            for b in range(3):
                p_ref[b, q : q + 8, base + TILE : base + TILE + wide] = acc[8 * b : 8 * b + 8]

    def carry(ref, rows, width):
        for k in range(width):
            ref[:rows, at(TILES + k)] = turned(ref[:rows, at(k)], -1)
            ref[:rows, at(-1 - k)] = turned(ref[:rows, at(TILES - 1 - k)], 1)

    for n in range(NCHUNK):
        layer1(*chunks[n])
    carry(h1_ref, R1 * CH, 2)
    for n in (1, 2, 3, 4, 5, 6, 7, 8, 0):
        layer2(*chunks[n])
    carry(h2_ref, R2 * CH, 4)
    for n in (3, 4, 5, 6, 7, 8, 0, 1, 2):
        layer3(*chunks[n])
        layer4(*chunks[n])
    p_ref[0, :, 0:TILE] = pltpu.roll(p_ref[0, :, TILES * TILE : (TILES + 1) * TILE], 1, 1)
    p_ref[2, :, (TILES + 1) * TILE : (TILES + 2) * TILE] = pltpu.roll(p_ref[2, :, TILE : 2 * TILE], TILE - 1, 1)
    tiles = [
        p_ref[0, :, k * TILE : (k + 1) * TILE]
        + p_ref[1, :, (k + 1) * TILE : (k + 2) * TILE]
        + p_ref[2, :, (k + 2) * TILE : (k + 3) * TILE]
        for k in range(TILES)
    ]
    col = iota((3 * TILE, 1), 0)
    tau = jnp.where(col < SEG, TILES * (col & 15) + (col >> 4), -1)
    order = onehot(tau == iota((1, TS), 1) + HALO)
    copies = []
    firsts, seconds = transposed(tiles[0:8]), transposed(tiles[8:16])
    for c in range(CL):
        third = pltpu.roll(tiles[16], TILE - 16 * c, 1) if c else tiles[16]
        noise = jnp.concatenate([firsts[c], seconds[c], third], axis=1)
        top = noise.astype(BF)
        rest = (noise - top.astype(F32)).astype(BF)
        both = dot(jnp.concatenate([top, rest], axis=0), order)
        out_ref[c] = stack_ref[c].astype(F32) - (both[0:MB] + both[MB:])
        copy = pltpu.make_async_copy(out_ref.at[c], out_hbm.at[c], sems.at[c])
        copy.start()
        copies.append(copy)
    for copy in copies:
        copy.wait()


def call(kernel, outs, scratch=(), smem=0, n=0, loose=0, name=None, limit=20, where=None):
    specs = [pl.BlockSpec(memory_space=pltpu.SMEM) for _ in range(smem)]
    specs += [pl.BlockSpec(memory_space=pltpu.VMEM) for _ in range(n)]
    specs += [pl.BlockSpec(memory_space=pl.ANY) for _ in range(loose)]
    number = len(outs) if isinstance(outs, tuple) else 1
    out_specs = tuple(pl.BlockSpec(memory_space=space) for space in where or (pltpu.VMEM,) * number)
    return pl.pallas_call(
        kernel,
        out_shape=outs,
        in_specs=specs,
        out_specs=out_specs if isinstance(outs, tuple) else out_specs[0],
        scratch_shapes=list(scratch),
        compiler_params=pltpu.CompilerParams(vmem_limit_bytes=limit * 2**20),
        name=name,
    )


def shape(*dims, dtype=BF):
    return pltpu.VMEM(dims, dtype)


def far(x):
    return pltpu.with_memory_space_constraint(x, pltpu.HBM)


def near(x):
    return pltpu.with_memory_space_constraint(x, pltpu.VMEM)


def build_send(dest, cell, traces):
    outs = (jax.ShapeDtypeStruct((OWNERS, PAY, TILE), BF), jax.ShapeDtypeStruct((8, 128), F32))
    scratch = [pltpu.VMEM((OWNERS, PAY, TILE), BF), pltpu.SemaphoreType.DMA((4,))]
    scratch += [pltpu.VMEM((1, COUNT), jnp.int32), pltpu.VMEM((1, COUNT), jnp.int32), pltpu.VMEM((COUNT, TS), BF)]
    scratch += [pltpu.SemaphoreType.DMA((3,))]
    return call(send_kernel, outs, scratch, loose=3, name="send", where=(pl.ANY, pltpu.VMEM))(
        far(dest), far(cell), far(traces)
    )


def build_weights(w_first, w_mid, w_last, bias, token):
    outs = (shape(R1 * CH, KDIM), shape(GROUP * CH, KDIM), shape(GROUP * CH, KDIM), shape(24, 160))
    return call(weights_kernel, outs, n=5, name="weights")(w_first, w_mid, w_last, bias, token)


def build_stack(recv, w1, pos):
    outs = (shape(CL, MB, TS), shape(MB, MB), shape(MB, MB))
    return call(stack_kernel, outs, n=1, loose=2, name="stack")(near(recv), w1, pos)


def reorder(stack, low, high):
    outs = (shape(MB, LANES), shape(HALO, LANES), shape(HALO, LANES))
    return call(swap_kernel, outs, n=3, name="reorder")(near(stack), near(low), near(high))


def convolve(pos, core, low, high, stack, weights):
    scratch = [
        pltpu.VMEM((CL, MB, TS), F32),
        pltpu.SemaphoreType.DMA((CL,)),
        pltpu.VMEM((80, 20 * TILE), BF),
        pltpu.VMEM((80 * CH, EXT), BF),
        pltpu.VMEM((R2 * CH, EXT), BF),
        pltpu.VMEM((R3 * CH, WIDE), BF),
        pltpu.VMEM((3, MB, 20 * TILE), F32),
        pltpu.VMEM((3, CH, WIDE), BF),
    ]
    return call(conv_kernel, jax.ShapeDtypeStruct((CL, MB, TS), F32), scratch, smem=1, n=8, name="conv", limit=40, where=(pl.ANY,))(
        pos, near(core), near(low), near(high), near(stack), *[near(w) for w in weights]
    )


def neighbours(low_edge, high_edge, axis):
    count = lax.axis_size(axis)
    up = [(i, i + 1) for i in range(count - 1)]
    down = [(b, a) for a, b in up]
    return lax.ppermute(high_edge, axis, up), lax.ppermute(low_edge, axis, down)


def shards(traces, dest, cell, w_first, w_mid, w_last, bias):
    send, token = build_send(dest.reshape(1, COUNT), cell.reshape(1, COUNT), traces)
    recv = lax.all_to_all(send, ("offset", "mid"), split_axis=0, concat_axis=0, tiled=True)
    weights = build_weights(w_first, w_mid, w_last, bias, token)
    pos = jnp.stack([lax.axis_index("mid"), lax.axis_index("tm")]).astype(jnp.int32)
    stack, left, right = build_stack(recv, weights[0], pos)
    low, high = neighbours(left, right, "tm")
    core, first, last = reorder(stack, low, high)
    below, above = neighbours(first, last, "mid")
    return convolve(pos, core, below, above, stack, weights)


def solution(mesh):
    rows = P(("offset", "mid"), "tm")
    column = P(("offset", "mid"), None)
    placed = (rows, column, column, P(), P(), P(), P())
    return jax.shard_map(
        shards, mesh=mesh, in_specs=placed, out_specs=P("offset", "mid", "tm"), check_vma=False
    )
```

```python
import functools

import jax
import jax.numpy as jnp
from jax import lax
from jax.experimental import pallas as pl
from jax.experimental.pallas import tpu as pltpu
from jax.sharding import PartitionSpec as P

BF = jnp.bfloat16
F32 = jnp.float32
OWNERS = 32
SLOTS = 64
COUNT = 1024
TS = 256
CL = 8
MB = 64
HALO = 8
SEG = TS + 2 * HALO
LANES = CL * SEG
TILE = 128
TILES = 17
CHUNK = 2 * TILE
NCHUNK = 9
WIDE = CHUNK * NCHUNK
LEAD = 4
EXT = (LEAD + 22) * TILE
CH = 16
R1, R2, R3 = 78, 74, 66
TAPS = 240
KDIM = 256
GROUP = 3
EXTRA = 8
PAY = 2 * SLOTS + EXTRA


def slots_of(rows, groups):
    return [r for g in range(groups) for r in range(g, rows, groups)]


ORDER1 = slots_of(R1, 2)
ORDER2 = slots_of(R2, 4)
SLOT2 = {r: s for s, r in enumerate(ORDER2)}
INNER = [(4, 35), (43, 74)]
EDGES = [(0, 4), (35, 43), (74, 78)]


def iota(shape, dim):
    return lax.broadcasted_iota(jnp.int32, shape, dim)


def onehot(mask):
    return jnp.where(mask, 1.0, 0.0).astype(BF)


def dot(a, b):
    return jnp.dot(a, b, preferred_element_type=F32)


def dot_t(a, b):
    return lax.dot_general(a, b, (((1,), (1,)), ((), ())), preferred_element_type=F32)


def send_kernel(dest_hbm, cell_hbm, traces_hbm, out_hbm, token_ref, out_ref, sems, dest_ref, cell_ref, traces_ref, ins):
    loads = [
        pltpu.make_async_copy(source, target, ins.at[n])
        for n, (source, target) in enumerate(((dest_hbm, dest_ref), (cell_hbm, cell_ref), (traces_hbm, traces_ref)))
    ]
    for load in loads:
        load.start()
    for load in loads[:2]:
        load.wait()
    dest = dest_ref[...]
    cell = cell_ref[...]
    width = 256
    blocks = COUNT // width
    owner = iota((OWNERS, width), 0)
    hots = [owner == dest[:, n * width : (n + 1) * width] for n in range(blocks)]
    upper = onehot(iota((width, width), 0) < iota((width, width), 1))
    before = dot(jnp.concatenate([onehot(hot) for hot in hots], axis=0), upper)
    ranks = []
    offset = jnp.zeros((OWNERS, 1), F32)
    for n, hot in enumerate(hots):
        part = before[n * OWNERS : (n + 1) * OWNERS]
        ranks.append(jnp.sum(jnp.where(hot, part + offset, 0.0), axis=0, keepdims=True))
        offset = offset + jnp.sum(jnp.where(hot, 1.0, 0.0), axis=1, keepdims=True)
    rank = jnp.concatenate(ranks, axis=1)
    place = dest * SLOTS + rank.astype(jnp.int32)
    high = (cell >> 5) + 1
    low = cell & 31
    row = iota((16, COUNT), 0)
    meta = jnp.where(row == 0, high, jnp.where(row == 1, low, 0)).astype(F32).astype(BF)
    loads[2].wait()
    traces = traces_ref[...]
    blank = jnp.zeros((EXTRA, TILE - SLOTS), F32)
    step = 8
    copies = []
    for o in range(0, OWNERS, step):
        slot = iota((step * SLOTS, COUNT), 0) + o * SLOTS
        placing = onehot(slot == place)
        rows = dot(placing, traces).astype(BF)
        extra = dot_t(meta, placing)
        for k in range(step):
            out_ref[o + k, 0:SLOTS, :] = rows[k * SLOTS : (k + 1) * SLOTS, 0:TILE]
            out_ref[o + k, SLOTS : 2 * SLOTS, :] = rows[k * SLOTS : (k + 1) * SLOTS, TILE:]
            part = extra[0:EXTRA, k * SLOTS : (k + 1) * SLOTS]
            out_ref[o + k, 2 * SLOTS : PAY, :] = jnp.concatenate([part, blank], axis=1).astype(BF)
        copy = pltpu.make_async_copy(out_ref.at[o : o + step], out_hbm.at[o : o + step], sems.at[o // step])
        copy.start()
        copies.append(copy)
    token_ref[...] = jnp.zeros(token_ref.shape, F32) + rank[:, 0:128]
    for copy in copies:
        copy.wait()


def weights_kernel(first_ref, mid_ref, last_ref, bias_ref, token_ref, w1_ref, w2_ref, w3_ref, w4_ref):
    bias = 0.5 * bias_ref[...]
    parts = []
    for _ in range(3):
        part = bias.astype(BF)
        parts.append(part)
        bias = bias - part.astype(F32)

    def bias_columns(spread, layer):
        row = iota((16, CH), 0)
        lines = jnp.zeros((16, CH), F32)
        for e in range(3):
            lines = jnp.where(row == e, parts[e][layer : layer + 1].astype(F32), lines)
        spreaded = dot_t(spread, lines.astype(BF)).astype(BF)
        return dot(spreaded, onehot(iota((16, KDIM), 1) == iota((16, KDIM), 0) + TAPS))

    step = 6 * CH
    first = first_ref[...]
    c = iota((step, KDIM), 1)
    b = jnp.where(c >= 80, 1, 0) + jnp.where(c >= 160, 1, 0)
    m = jnp.where(c < TAPS, c - 80 * b, -100)
    ck = iota((9, KDIM), 1)
    bk = jnp.where(ck >= 80, 1, 0) + jnp.where(ck >= 160, 1, 0)
    spread = onehot((iota((step, CH), 0) & (CH - 1)) == iota((step, CH), 1))
    base = dot(spread, first).astype(BF)
    picked = [0.5 * dot(base, onehot(iota((9, KDIM), 0) == 3 * a + bk)) for a in range(3)]
    other = bias_columns(spread, 0)
    for n in range(R1 * CH // step):
        r = (iota((step, KDIM), 0) >> 4) + 6 * n
        r = jnp.where(r < R1 // 2, 2 * r, 2 * r - (R1 - 1))
        total = other
        for a in range(3):
            total = jnp.where(m - r == a, picked[a], total)
        w1_ref[n * step : (n + 1) * step, :] = total.astype(BF)
    rows = GROUP * CH
    spread = onehot((iota((rows, CH), 0) & (CH - 1)) == iota((rows, CH), 1))
    c = iota((rows, KDIM), 1)
    b = jnp.where(c >= 80, 1, 0) + jnp.where(c >= 160, 1, 0)
    delta = jnp.where(c < TAPS, ((c - 80 * b) >> 4) - (iota((rows, KDIM), 0) >> 4), -100)
    ck = iota((144, KDIM), 1)
    bk = jnp.where(ck >= 80, 1, 0) + jnp.where(ck >= 160, 1, 0)
    for layer, out_ref in ((0, w2_ref), (1, w3_ref)):
        base = dot(spread, mid_ref[layer]).astype(BF)
        total = bias_columns(spread, layer + 1)
        for a in range(3):
            pick = onehot(iota((144, KDIM), 0) == (3 * a + bk) * CH + (ck & 15))
            total = jnp.where(delta == a, 0.5 * dot(base, pick), total)
        out_ref[...] = total.astype(BF)
    last = jnp.broadcast_to(last_ref[...], (24, 144))
    delta = (iota((24, 160), 1) >> 4) - (iota((24, 160), 0) & 7)
    tap = iota((24, 160), 0) >> 3
    col = iota((144, 160), 1) & 15
    total = jnp.zeros((24, 160), F32)
    for b in range(3):
        for a in range(3):
            line = dot(last, onehot(iota((144, 160), 0) == (3 * a + b) * CH + col))
            total = jnp.where((delta == a) & (tap == b), line, total)
    w4_ref[...] = total.astype(BF)


def stack_kernel(recv_ref, w1_ref, pos_ref, out_ref, left_ref, right_ref):
    cells = []
    for s in range(OWNERS):
        extra = recv_ref[s, 2 * SLOTS : PAY, 0:SLOTS].astype(F32)
        cells.append((extra[0:1] - 1.0) * 32.0 + extra[1:2])
    cell = jnp.concatenate(cells, axis=1).astype(jnp.int32)
    total = OWNERS * SLOTS
    rows = jnp.concatenate(
        [recv_ref[:, 0:SLOTS, :].reshape(total, TILE), recv_ref[:, SLOTS : 2 * SLOTS, :].reshape(total, TILE)], axis=1
    )
    lefts, rights = [], []
    step = 4
    for c in range(0, CL, step):
        hit = jnp.where(iota((step * MB, total), 0) + c * MB == cell, 1.0, 0.0)
        fold = jnp.maximum(jnp.sum(hit, axis=1, keepdims=True), 1.0)
        part = dot(hit.astype(BF), rows) / fold
        for k in range(step):
            piece = part[k * MB : (k + 1) * MB]
            out_ref[c + k] = piece.astype(BF)
            lefts.append(piece[:, 0:HALO])
            rights.append(piece[:, TS - HALO :])
    left_ref[...] = jnp.concatenate(lefts, axis=1).astype(BF)
    right_ref[...] = jnp.concatenate(rights, axis=1).astype(BF)


def transposed(blocks):
    group = iota(blocks[0].shape, 1) >> 4
    blocks = list(blocks)
    for bit in (1, 2, 4):
        keep = (group & bit) == 0
        for i in range(8):
            if i & bit == 0:
                a, b = blocks[i], blocks[i | bit]
                blocks[i] = jnp.where(keep, a, pltpu.roll(b, 16 * bit, 1))
                blocks[i | bit] = jnp.where(keep, pltpu.roll(a, TILE - 16 * bit, 1), b)
    return blocks


def swap_kernel(stack_ref, low_ref, high_ref, out_ref, first_ref, last_ref):
    side = jnp.concatenate([low_ref[...].astype(F32), high_ref[...].astype(F32)], axis=1)
    owner = (iota((MB, TILE), 1) >> 3) & 7
    rows = TS + TILE
    row = iota((rows, 1), 0)
    tau = row + HALO
    tau = jnp.where(row >= TS, row & 7, tau)
    tau = jnp.where(row >= TS + TILE // 2, (row & 7) + TS + HALO, tau)
    col = iota((1, 3 * TILE), 1)
    order = onehot(tau == TILES * (col & 15) + jnp.minimum(col >> 4, TILES - 1))
    full = []
    for c in range(CL):
        full.append(jnp.concatenate([stack_ref[c], jnp.where(owner == c, side, 0.0).astype(BF)], axis=1))
    mixed = dot(jnp.concatenate(full, axis=0), order)
    for half in range(2):
        blocks = [mixed[c * MB : (c + 1) * MB, half * TILE : (half + 1) * TILE] for c in range(CL)]
        for k, tile in enumerate(transposed(blocks)):
            k = 8 * half + k
            out_ref[:, k * TILE : (k + 1) * TILE] = tile.astype(BF)
    lane = iota((MB, TILE), 1) >> 4
    tile = jnp.zeros((MB, TILE), F32)
    for c in range(CL):
        tile = jnp.where(lane == c, mixed[c * MB : (c + 1) * MB, 2 * TILE :], tile)
    out_ref[:, 16 * TILE :] = tile.astype(BF)
    first_ref[...] = out_ref[0:HALO, :]
    last_ref[...] = out_ref[MB - HALO : MB, :]


def gelu_half(h):
    c0 = 2.0 * 0.7978845608028654
    c1 = 8.0 * 0.7978845608028654 * 0.044715
    return h + h * jnp.tanh(h * (c0 + c1 * (h * h)))


def turned(block, shift):
    return pltpu.roll(block, shift % TILE, 1)


def at(k):
    return slice((LEAD + k) * TILE, (LEAD + k + 1) * TILE)


CHUNKS = [(k * CHUNK, min(CHUNK, LANES - k * CHUNK)) for k in range(NCHUNK)]


def valid(tm):
    lane = iota((CH, WIDE), 1)
    t = TILES * ((lane & 127) & 15) + (lane >> 7) - HALO + tm * TS
    return jnp.where((t >= 0) & (t < 4 * TS), 1.0, 0.0)


def fill(x_ref, image):
    x_ref[:, TILE : TILE + LANES] = image.astype(BF)
    x_ref[:, 0:TILE] = pltpu.roll(image[:, 16 * TILE :], 1, 1).astype(BF)
    for k in range(2):
        x_ref[:, (18 + k) * TILE : (19 + k) * TILE] = pltpu.roll(image[:, k * TILE : (k + 1) * TILE], TILE - 1, 1).astype(BF)


def finish(acc, row, base, wide, into_ref, slot, lead, mask_ref):
    which = 1 if row < 0 else (2 if row >= MB else 0)
    g = gelu_half(acc).astype(BF) * mask_ref[which, :, base : base + wide]
    into_ref[slot * CH : (slot + 1) * CH, base + lead * TILE : base + lead * TILE + wide] = g


def layer1(base, wide, x_ref, w1_ref, into_ref, mask_ref, runs):
    x = [x_ref[:, base + b * TILE : base + b * TILE + wide] for b in range(3)]
    x = jnp.concatenate(x + [jnp.ones((KDIM - TAPS, wide), BF)], axis=0)
    for low, high in runs:
        for s0 in range(low, high, 11):
            count = min(11, high - s0)
            acc = dot(w1_ref[s0 * CH : (s0 + count) * CH, :], x)
            for j in range(count):
                row = ORDER1[s0 + j] - 7
                finish(acc[j * CH : (j + 1) * CH], row, base, wide, into_ref, s0 + j, LEAD, mask_ref)


def carry(ref, runs, width):
    for low, high in runs:
        rows = slice(low * CH, high * CH)
        for k in range(width):
            ref[rows, at(TILES + k)] = turned(ref[rows, at(k)], -1)
            ref[rows, at(-1 - k)] = turned(ref[rows, at(TILES - 1 - k)], 1)


def inner_kernel(pos_ref, core_ref, w1_ref, h1_ref, x_ref, mask_ref):
    mask_ref[0] = valid(pos_ref[1]).astype(BF)
    blank = jnp.zeros((HALO, LANES), F32)
    fill(x_ref, jnp.concatenate([blank, core_ref[...].astype(F32), blank], axis=0))
    for base, wide in CHUNKS:
        layer1(base, wide, x_ref, w1_ref, h1_ref, mask_ref, INNER)
    carry(h1_ref, INNER, 2)


def conv_kernel(pos_ref, core_ref, low_ref, high_ref, inner_ref, stack_ref, w1_ref, w2_ref, w3_ref, w4_ref, out_hbm,
                out_ref, sems, x_ref, h1_ref, h2_ref, h3_ref, p_ref, mask_ref):
    mid = pos_ref[0]
    keep = valid(pos_ref[1])
    mask_ref[0] = keep.astype(BF)
    mask_ref[1] = (keep * jnp.where(mid > 0, 1.0, 0.0)).astype(BF)
    mask_ref[2] = (keep * jnp.where(mid < 7, 1.0, 0.0)).astype(BF)
    fill(x_ref, jnp.concatenate([low_ref[...].astype(F32), core_ref[...].astype(F32), high_ref[...].astype(F32)], axis=0))
    chunks = CHUNKS
    h1_ref[R1 * CH :, :] = jnp.zeros((2 * CH, EXT), BF)

    def rows1(s0, lanes):
        pieces, slot = [], s0
        while slot < s0 + 5:
            inside = any(low <= slot < high for low, high in INNER)
            stop = slot
            while stop < s0 + 5 and any(low <= stop < high for low, high in INNER) == inside:
                stop += 1
            pieces.append((inner_ref if inside else h1_ref)[slot * CH : stop * CH, lanes])
            slot = stop
        return pieces

    def rows2(s0, lanes):
        return [h2_ref[s0 * CH : (s0 + 5) * CH, lanes]]

    def window(rows, s0, base, wide, d):
        taps = []
        for b in range(3):
            lane = base + (LEAD + (b - 1) * d) * TILE
            taps += rows(s0, slice(lane, lane + wide))
        return jnp.concatenate(taps + [jnp.ones((KDIM - TAPS, wide), BF)], axis=0)

    def layer2(base, wide):
        for s0 in range(0, R1 - 2, GROUP):
            acc = dot(w2_ref[...], window(rows1, s0, base, wide, 2))
            for j in range(GROUP):
                if s0 + j < R1 and ORDER1[s0 + j] < R2:
                    q = ORDER1[s0 + j]
                    finish(acc[j * CH : (j + 1) * CH], q - 5, base, wide, h2_ref, SLOT2[q], LEAD, mask_ref)

    def layer3(base, wide):
        for s0 in range(0, R2 - 2, GROUP):
            acc = dot(w3_ref[...], window(rows2, s0, base, wide, 4))
            for j in range(GROUP):
                if ORDER2[s0 + j] < R3:
                    q = ORDER2[s0 + j]
                    finish(acc[j * CH : (j + 1) * CH], q - 1, base, wide, h3_ref, q, 0, mask_ref)

    def layer4(base, wide):
        for q in range(0, MB, 8):
            acc = dot(w4_ref[...], h3_ref[q * CH : (q + 10) * CH, base : base + wide])
            for b in range(3):
                p_ref[b, q : q + 8, base + TILE : base + TILE + wide] = acc[8 * b : 8 * b + 8]

    for n in range(NCHUNK):
        layer1(*chunks[n], x_ref, w1_ref, h1_ref, mask_ref, EDGES)
    carry(h1_ref, EDGES, 2)
    for n in (1, 2, 3, 4, 5, 6, 7, 8, 0):
        layer2(*chunks[n])
    carry(h2_ref, [(0, R2)], 4)
    for n in (3, 4, 5, 6, 7, 8, 0, 1, 2):
        layer3(*chunks[n])
        layer4(*chunks[n])
    p_ref[0, :, 0:TILE] = pltpu.roll(p_ref[0, :, TILES * TILE : (TILES + 1) * TILE], 1, 1)
    p_ref[2, :, (TILES + 1) * TILE : (TILES + 2) * TILE] = pltpu.roll(p_ref[2, :, TILE : 2 * TILE], TILE - 1, 1)
    tiles = [
        p_ref[0, :, k * TILE : (k + 1) * TILE]
        + p_ref[1, :, (k + 1) * TILE : (k + 2) * TILE]
        + p_ref[2, :, (k + 2) * TILE : (k + 3) * TILE]
        for k in range(TILES)
    ]
    col = iota((3 * TILE, 1), 0)
    tau = jnp.where(col < SEG, TILES * (col & 15) + (col >> 4), -1)
    order = onehot(tau == iota((1, TS), 1) + HALO)
    copies = []
    firsts, seconds = transposed(tiles[0:8]), transposed(tiles[8:16])
    for c in range(CL):
        third = pltpu.roll(tiles[16], TILE - 16 * c, 1) if c else tiles[16]
        noise = jnp.concatenate([firsts[c], seconds[c], third], axis=1)
        top = noise.astype(BF)
        rest = (noise - top.astype(F32)).astype(BF)
        both = dot(jnp.concatenate([top, rest], axis=0), order)
        out_ref[c] = stack_ref[c].astype(F32) - (both[0:MB] + both[MB:])
        copy = pltpu.make_async_copy(out_ref.at[c], out_hbm.at[c], sems.at[c])
        copy.start()
        copies.append(copy)
    for copy in copies:
        copy.wait()


def call(kernel, outs, scratch=(), smem=0, n=0, loose=0, name=None, limit=20, where=None):
    specs = [pl.BlockSpec(memory_space=pltpu.SMEM) for _ in range(smem)]
    specs += [pl.BlockSpec(memory_space=pltpu.VMEM) for _ in range(n)]
    specs += [pl.BlockSpec(memory_space=pl.ANY) for _ in range(loose)]
    number = len(outs) if isinstance(outs, tuple) else 1
    out_specs = tuple(pl.BlockSpec(memory_space=space) for space in where or (pltpu.VMEM,) * number)
    return pl.pallas_call(
        kernel,
        out_shape=outs,
        in_specs=specs,
        out_specs=out_specs if isinstance(outs, tuple) else out_specs[0],
        scratch_shapes=list(scratch),
        compiler_params=pltpu.CompilerParams(vmem_limit_bytes=limit * 2**20),
        name=name,
    )


def shape(*dims, dtype=BF):
    return pltpu.VMEM(dims, dtype)


def far(x):
    return pltpu.with_memory_space_constraint(x, pltpu.HBM)


def near(x):
    return pltpu.with_memory_space_constraint(x, pltpu.VMEM)


def build_send(dest, cell, traces):
    outs = (jax.ShapeDtypeStruct((OWNERS, PAY, TILE), BF), jax.ShapeDtypeStruct((8, 128), F32))
    scratch = [pltpu.VMEM((OWNERS, PAY, TILE), BF), pltpu.SemaphoreType.DMA((4,))]
    scratch += [pltpu.VMEM((1, COUNT), jnp.int32), pltpu.VMEM((1, COUNT), jnp.int32), pltpu.VMEM((COUNT, TS), BF)]
    scratch += [pltpu.SemaphoreType.DMA((3,))]
    return call(send_kernel, outs, scratch, loose=3, name="send", where=(pl.ANY, pltpu.VMEM))(
        far(dest), far(cell), far(traces)
    )


def build_weights(w_first, w_mid, w_last, bias, token):
    outs = (shape(R1 * CH, KDIM), shape(GROUP * CH, KDIM), shape(GROUP * CH, KDIM), shape(24, 160))
    return call(weights_kernel, outs, n=5, name="weights")(w_first, w_mid, w_last, bias, token)


def build_stack(recv, w1, pos):
    outs = (shape(CL, MB, TS), shape(MB, MB), shape(MB, MB))
    return call(stack_kernel, outs, n=1, loose=2, name="stack")(near(recv), w1, pos)


def reorder(stack, low, high):
    outs = (shape(MB, LANES), shape(HALO, LANES), shape(HALO, LANES))
    return call(swap_kernel, outs, n=3, name="reorder")(near(stack), near(low), near(high))


def inside(pos, core, w1):
    scratch = [pltpu.VMEM((80, 20 * TILE), BF), pltpu.VMEM((3, CH, WIDE), BF)]
    return call(inner_kernel, shape(R1 * CH, EXT), scratch, smem=1, n=2, name="inner")(pos, near(core), near(w1))


def convolve(pos, core, low, high, inner, stack, weights):
    scratch = [
        pltpu.VMEM((CL, MB, TS), F32),
        pltpu.SemaphoreType.DMA((CL,)),
        pltpu.VMEM((80, 20 * TILE), BF),
        pltpu.VMEM((80 * CH, EXT), BF),
        pltpu.VMEM((R2 * CH, EXT), BF),
        pltpu.VMEM((R3 * CH, WIDE), BF),
        pltpu.VMEM((3, MB, 20 * TILE), F32),
        pltpu.VMEM((3, CH, WIDE), BF),
    ]
    return call(conv_kernel, jax.ShapeDtypeStruct((CL, MB, TS), F32), scratch, smem=1, n=9, name="conv", limit=40, where=(pl.ANY,))(
        pos, near(core), near(low), near(high), near(inner), near(stack), *[near(w) for w in weights]
    )


def neighbours(low_edge, high_edge, axis):
    count = lax.axis_size(axis)
    up = [(i, i + 1) for i in range(count - 1)]
    down = [(b, a) for a, b in up]
    return lax.ppermute(high_edge, axis, up), lax.ppermute(low_edge, axis, down)


def shards(traces, dest, cell, w_first, w_mid, w_last, bias):
    send, token = build_send(dest.reshape(1, COUNT), cell.reshape(1, COUNT), traces)
    recv = lax.all_to_all(send, ("offset", "mid"), split_axis=0, concat_axis=0, tiled=True)
    weights = build_weights(w_first, w_mid, w_last, bias, token)
    pos = jnp.stack([lax.axis_index("mid"), lax.axis_index("tm")]).astype(jnp.int32)
    stack, left, right = build_stack(recv, weights[0], pos)
    low, high = neighbours(left, right, "tm")
    core, first, last = reorder(stack, low, high)
    below, above = neighbours(first, last, "mid")
    inner = inside(pos, core, weights[0])
    return convolve(pos, core, below, above, inner, stack, weights)


def solution(mesh):
    rows = P(("offset", "mid"), "tm")
    column = P(("offset", "mid"), None)
    placed = (rows, column, column, P(), P(), P(), P())
    return jax.shard_map(
        shards, mesh=mesh, in_specs=placed, out_specs=P("offset", "mid", "tm"), check_vma=False
    )
```

```python
import functools

import jax
import jax.numpy as jnp
from jax import lax
from jax.experimental import pallas as pl
from jax.experimental.pallas import tpu as pltpu
from jax.sharding import PartitionSpec as P

BF = jnp.bfloat16
F32 = jnp.float32
OWNERS = 32
SLOTS = 64
COUNT = 1024
TS = 256
CL = 8
MB = 64
HALO = 8
SEG = TS + 2 * HALO
LANES = CL * SEG
TILE = 128
TILES = 17
CHUNK = 2 * TILE
NCHUNK = 9
WIDE = CHUNK * NCHUNK
LEAD = 4
EXT = (LEAD + 22) * TILE
CH = 16
R1, R2, R3 = 78, 74, 66
TAPS = 240
KDIM = 256
GROUP = 3
EXTRA = 8
PAY = 2 * SLOTS + EXTRA


def slots_of(rows, groups):
    return [r for g in range(groups) for r in range(g, rows, groups)]


ORDER1 = slots_of(R1, 2)
ORDER2 = slots_of(R2, 4)
SLOT2 = {r: s for s, r in enumerate(ORDER2)}
INNER = [(4, 35), (43, 74)]
EDGES = [(0, 4), (35, 43), (74, 78)]


def iota(shape, dim):
    return lax.broadcasted_iota(jnp.int32, shape, dim)


def onehot(mask):
    return jnp.where(mask, 1.0, 0.0).astype(BF)


def dot(a, b):
    return jnp.dot(a, b, preferred_element_type=F32)


def dot_t(a, b):
    return lax.dot_general(a, b, (((1,), (1,)), ((), ())), preferred_element_type=F32)


def send_kernel(dest_hbm, cell_hbm, traces_hbm, out_hbm, token_ref, out_ref, sems, dest_ref, cell_ref, traces_ref, ins):
    loads = [
        pltpu.make_async_copy(source, target, ins.at[n])
        for n, (source, target) in enumerate(((dest_hbm, dest_ref), (cell_hbm, cell_ref), (traces_hbm, traces_ref)))
    ]
    for load in loads:
        load.start()
    for load in loads[:2]:
        load.wait()
    dest = dest_ref[...]
    cell = cell_ref[...]
    width = 256
    blocks = COUNT // width
    owner = iota((OWNERS, width), 0)
    hots = [owner == dest[:, n * width : (n + 1) * width] for n in range(blocks)]
    upper = onehot(iota((width, width), 0) < iota((width, width), 1))
    before = dot(jnp.concatenate([onehot(hot) for hot in hots], axis=0), upper)
    ranks = []
    offset = jnp.zeros((OWNERS, 1), F32)
    for n, hot in enumerate(hots):
        part = before[n * OWNERS : (n + 1) * OWNERS]
        ranks.append(jnp.sum(jnp.where(hot, part + offset, 0.0), axis=0, keepdims=True))
        offset = offset + jnp.sum(jnp.where(hot, 1.0, 0.0), axis=1, keepdims=True)
    rank = jnp.concatenate(ranks, axis=1)
    place = dest * SLOTS + rank.astype(jnp.int32)
    high = (cell >> 5) + 1
    low = cell & 31
    row = iota((16, COUNT), 0)
    meta = jnp.where(row == 0, high, jnp.where(row == 1, low, 0)).astype(F32).astype(BF)
    loads[2].wait()
    traces = traces_ref[...]
    blank = jnp.zeros((EXTRA, TILE - SLOTS), F32)
    step = 8
    copies = []
    for o in range(0, OWNERS, step):
        slot = iota((step * SLOTS, COUNT), 0) + o * SLOTS
        placing = onehot(slot == place)
        rows = dot(placing, traces).astype(BF)
        extra = dot_t(meta, placing)
        for k in range(step):
            out_ref[o + k, 0:SLOTS, :] = rows[k * SLOTS : (k + 1) * SLOTS, 0:TILE]
            out_ref[o + k, SLOTS : 2 * SLOTS, :] = rows[k * SLOTS : (k + 1) * SLOTS, TILE:]
            part = extra[0:EXTRA, k * SLOTS : (k + 1) * SLOTS]
            out_ref[o + k, 2 * SLOTS : PAY, :] = jnp.concatenate([part, blank], axis=1).astype(BF)
        copy = pltpu.make_async_copy(out_ref.at[o : o + step], out_hbm.at[o : o + step], sems.at[o // step])
        copy.start()
        copies.append(copy)
    token_ref[...] = jnp.zeros(token_ref.shape, F32) + rank[:, 0:128]
    for copy in copies:
        copy.wait()


def weights_kernel(first_ref, mid_ref, last_ref, bias_ref, token_ref, w1_ref, w2_ref, w3_ref, w4_ref):
    bias = 0.5 * bias_ref[...]
    parts = []
    for _ in range(3):
        part = bias.astype(BF)
        parts.append(part)
        bias = bias - part.astype(F32)

    def bias_columns(spread, layer):
        row = iota((16, CH), 0)
        lines = jnp.zeros((16, CH), F32)
        for e in range(3):
            lines = jnp.where(row == e, parts[e][layer : layer + 1].astype(F32), lines)
        spreaded = dot_t(spread, lines.astype(BF)).astype(BF)
        return dot(spreaded, onehot(iota((16, KDIM), 1) == iota((16, KDIM), 0) + TAPS))

    step = 6 * CH
    first = first_ref[...]
    c = iota((step, KDIM), 1)
    b = jnp.where(c >= 80, 1, 0) + jnp.where(c >= 160, 1, 0)
    m = jnp.where(c < TAPS, c - 80 * b, -100)
    ck = iota((9, KDIM), 1)
    bk = jnp.where(ck >= 80, 1, 0) + jnp.where(ck >= 160, 1, 0)
    spread = onehot((iota((step, CH), 0) & (CH - 1)) == iota((step, CH), 1))
    base = dot(spread, first).astype(BF)
    picked = [0.5 * dot(base, onehot(iota((9, KDIM), 0) == 3 * a + bk)) for a in range(3)]
    other = bias_columns(spread, 0)
    for n in range(R1 * CH // step):
        r = (iota((step, KDIM), 0) >> 4) + 6 * n
        r = jnp.where(r < R1 // 2, 2 * r, 2 * r - (R1 - 1))
        total = other
        for a in range(3):
            total = jnp.where(m - r == a, picked[a], total)
        w1_ref[n * step : (n + 1) * step, :] = total.astype(BF)
    rows = GROUP * CH
    spread = onehot((iota((rows, CH), 0) & (CH - 1)) == iota((rows, CH), 1))
    c = iota((rows, KDIM), 1)
    b = jnp.where(c >= 80, 1, 0) + jnp.where(c >= 160, 1, 0)
    delta = jnp.where(c < TAPS, ((c - 80 * b) >> 4) - (iota((rows, KDIM), 0) >> 4), -100)
    ck = iota((144, KDIM), 1)
    bk = jnp.where(ck >= 80, 1, 0) + jnp.where(ck >= 160, 1, 0)
    for layer, out_ref in ((0, w2_ref), (1, w3_ref)):
        base = dot(spread, mid_ref[layer]).astype(BF)
        total = bias_columns(spread, layer + 1)
        for a in range(3):
            pick = onehot(iota((144, KDIM), 0) == (3 * a + bk) * CH + (ck & 15))
            total = jnp.where(delta == a, 0.5 * dot(base, pick), total)
        out_ref[...] = total.astype(BF)
    last = jnp.broadcast_to(last_ref[...], (24, 144))
    delta = (iota((24, 160), 1) >> 4) - (iota((24, 160), 0) & 7)
    tap = iota((24, 160), 0) >> 3
    col = iota((144, 160), 1) & 15
    total = jnp.zeros((24, 160), F32)
    for b in range(3):
        for a in range(3):
            line = dot(last, onehot(iota((144, 160), 0) == (3 * a + b) * CH + col))
            total = jnp.where((delta == a) & (tap == b), line, total)
    w4_ref[...] = total.astype(BF)


def stack_kernel(recv_ref, w1_ref, pos_ref, out_ref, left_ref, right_ref):
    cells = []
    for s in range(OWNERS):
        extra = recv_ref[s, 2 * SLOTS : PAY, 0:SLOTS].astype(F32)
        cells.append((extra[0:1] - 1.0) * 32.0 + extra[1:2])
    cell = jnp.concatenate(cells, axis=1).astype(jnp.int32)
    total = OWNERS * SLOTS
    rows = jnp.concatenate(
        [recv_ref[:, 0:SLOTS, :].reshape(total, TILE), recv_ref[:, SLOTS : 2 * SLOTS, :].reshape(total, TILE)], axis=1
    )
    lefts, rights = [], []
    step = 4
    for c in range(0, CL, step):
        hit = jnp.where(iota((step * MB, total), 0) + c * MB == cell, 1.0, 0.0)
        fold = jnp.maximum(jnp.sum(hit, axis=1, keepdims=True), 1.0)
        part = dot(hit.astype(BF), rows) / fold
        for k in range(step):
            piece = part[k * MB : (k + 1) * MB]
            out_ref[c + k] = piece.astype(BF)
            lefts.append(piece[:, 0:HALO])
            rights.append(piece[:, TS - HALO :])
    left_ref[...] = jnp.concatenate(lefts, axis=1).astype(BF)
    right_ref[...] = jnp.concatenate(rights, axis=1).astype(BF)


def transposed(blocks):
    group = iota(blocks[0].shape, 1) >> 4
    blocks = list(blocks)
    for bit in (1, 2, 4):
        keep = (group & bit) == 0
        for i in range(8):
            if i & bit == 0:
                a, b = blocks[i], blocks[i | bit]
                blocks[i] = jnp.where(keep, a, pltpu.roll(b, 16 * bit, 1))
                blocks[i | bit] = jnp.where(keep, pltpu.roll(a, TILE - 16 * bit, 1), b)
    return blocks


def swap_kernel(stack_ref, low_ref, high_ref, out_ref, first_ref, last_ref):
    side = jnp.concatenate([low_ref[...].astype(F32), high_ref[...].astype(F32)], axis=1)
    owner = (iota((MB, TILE), 1) >> 3) & 7
    rows = TS + TILE
    row = iota((rows, 1), 0)
    tau = row + HALO
    tau = jnp.where(row >= TS, row & 7, tau)
    tau = jnp.where(row >= TS + TILE // 2, (row & 7) + TS + HALO, tau)
    col = iota((1, 3 * TILE), 1)
    order = onehot(tau == TILES * (col & 15) + jnp.minimum(col >> 4, TILES - 1))
    full = []
    for c in range(CL):
        full.append(jnp.concatenate([stack_ref[c], jnp.where(owner == c, side, 0.0).astype(BF)], axis=1))
    mixed = dot(jnp.concatenate(full, axis=0), order)
    for half in range(2):
        blocks = [mixed[c * MB : (c + 1) * MB, half * TILE : (half + 1) * TILE] for c in range(CL)]
        for k, tile in enumerate(transposed(blocks)):
            k = 8 * half + k
            out_ref[:, k * TILE : (k + 1) * TILE] = tile.astype(BF)
    lane = iota((MB, TILE), 1) >> 4
    tile = jnp.zeros((MB, TILE), F32)
    for c in range(CL):
        tile = jnp.where(lane == c, mixed[c * MB : (c + 1) * MB, 2 * TILE :], tile)
    out_ref[:, 16 * TILE :] = tile.astype(BF)
    first_ref[...] = out_ref[0:HALO, :]
    last_ref[...] = out_ref[MB - HALO : MB, :]


def gelu_half(h):
    c0 = 2.0 * 0.7978845608028654
    c1 = 8.0 * 0.7978845608028654 * 0.044715
    return h + h * jnp.tanh(h * (c0 + c1 * (h * h)))


def turned(block, shift):
    return pltpu.roll(block, shift % TILE, 1)


def at(k):
    return slice((LEAD + k) * TILE, (LEAD + k + 1) * TILE)


CHUNKS = [(k * CHUNK, min(CHUNK, LANES - k * CHUNK)) for k in range(NCHUNK)]


def valid(tm):
    lane = iota((CH, WIDE), 1)
    t = TILES * ((lane & 127) & 15) + (lane >> 7) - HALO + tm * TS
    return jnp.where((t >= 0) & (t < 4 * TS), 1.0, 0.0)


def fill(x_ref, image):
    x_ref[:, TILE : TILE + LANES] = image.astype(BF)
    x_ref[:, 0:TILE] = pltpu.roll(image[:, 16 * TILE :], 1, 1).astype(BF)
    for k in range(2):
        x_ref[:, (18 + k) * TILE : (19 + k) * TILE] = pltpu.roll(image[:, k * TILE : (k + 1) * TILE], TILE - 1, 1).astype(BF)


def finish(acc, row, base, wide, into_ref, slot, lead, mask_ref):
    which = 1 if row < 0 else (2 if row >= MB else 0)
    g = gelu_half(acc).astype(BF) * mask_ref[which, :, base : base + wide]
    into_ref[slot * CH : (slot + 1) * CH, base + lead * TILE : base + lead * TILE + wide] = g


def layer1(base, wide, x_ref, w1_ref, into_ref, mask_ref, runs):
    x = [x_ref[:, base + b * TILE : base + b * TILE + wide] for b in range(3)]
    x = jnp.concatenate(x + [jnp.ones((KDIM - TAPS, wide), BF)], axis=0)
    slots = [s for low, high in runs for s in range(low, high)]
    for first in range(0, len(slots), 16):
        some = slots[first : first + 16]
        w = jnp.concatenate([w1_ref[s * CH : (s + 1) * CH, :] for s in some], axis=0)
        acc = dot(w, x)
        for j, s in enumerate(some):
            finish(acc[j * CH : (j + 1) * CH], ORDER1[s] - 7, base, wide, into_ref, s, LEAD, mask_ref)


def carry(ref, runs, width):
    for low, high in runs:
        rows = slice(low * CH, high * CH)
        for k in range(width):
            ref[rows, at(TILES + k)] = turned(ref[rows, at(k)], -1)
            ref[rows, at(-1 - k)] = turned(ref[rows, at(TILES - 1 - k)], 1)


def inner_kernel(pos_ref, core_ref, w1_ref, h1_ref, x_ref, mask_ref):
    mask_ref[0] = valid(pos_ref[1]).astype(BF)
    blank = jnp.zeros((HALO, LANES), F32)
    fill(x_ref, jnp.concatenate([blank, core_ref[...].astype(F32), blank], axis=0))
    for base, wide in CHUNKS:
        layer1(base, wide, x_ref, w1_ref, h1_ref, mask_ref, INNER)
    carry(h1_ref, INNER, 2)


def conv_kernel(pos_ref, core_ref, low_ref, high_ref, inner_ref, stack_ref, w1_ref, w2_ref, w3_ref, w4_ref, out_hbm,
                out_ref, sems, x_ref, h1_ref, h2_ref, h3_ref, p_ref, mask_ref):
    mid = pos_ref[0]
    keep = valid(pos_ref[1])
    mask_ref[0] = keep.astype(BF)
    mask_ref[1] = (keep * jnp.where(mid > 0, 1.0, 0.0)).astype(BF)
    mask_ref[2] = (keep * jnp.where(mid < 7, 1.0, 0.0)).astype(BF)
    fill(x_ref, jnp.concatenate([low_ref[...].astype(F32), core_ref[...].astype(F32), high_ref[...].astype(F32)], axis=0))
    chunks = CHUNKS
    h1_ref[R1 * CH :, :] = jnp.zeros((2 * CH, EXT), BF)

    def rows1(s0, lanes):
        pieces, slot = [], s0
        while slot < s0 + 5:
            inside = any(low <= slot < high for low, high in INNER)
            stop = slot
            while stop < s0 + 5 and any(low <= stop < high for low, high in INNER) == inside:
                stop += 1
            pieces.append((inner_ref if inside else h1_ref)[slot * CH : stop * CH, lanes])
            slot = stop
        return pieces

    def rows2(s0, lanes):
        return [h2_ref[s0 * CH : (s0 + 5) * CH, lanes]]

    def window(rows, s0, base, wide, d):
        taps = []
        for b in range(3):
            lane = base + (LEAD + (b - 1) * d) * TILE
            taps += rows(s0, slice(lane, lane + wide))
        return jnp.concatenate(taps + [jnp.ones((KDIM - TAPS, wide), BF)], axis=0)

    def layer2(base, wide):
        for s0 in range(0, R1 - 2, GROUP):
            acc = dot(w2_ref[...], window(rows1, s0, base, wide, 2))
            for j in range(GROUP):
                if s0 + j < R1 and ORDER1[s0 + j] < R2:
                    q = ORDER1[s0 + j]
                    finish(acc[j * CH : (j + 1) * CH], q - 5, base, wide, h2_ref, SLOT2[q], LEAD, mask_ref)

    def layer3(base, wide):
        for s0 in range(0, R2 - 2, GROUP):
            acc = dot(w3_ref[...], window(rows2, s0, base, wide, 4))
            for j in range(GROUP):
                if ORDER2[s0 + j] < R3:
                    q = ORDER2[s0 + j]
                    finish(acc[j * CH : (j + 1) * CH], q - 1, base, wide, h3_ref, q, 0, mask_ref)

    def layer4(base, wide):
        for q in range(0, MB, 8):
            acc = dot(w4_ref[...], h3_ref[q * CH : (q + 10) * CH, base : base + wide])
            for b in range(3):
                p_ref[b, q : q + 8, base + TILE : base + TILE + wide] = acc[8 * b : 8 * b + 8]

    for n in range(NCHUNK):
        layer1(*chunks[n], x_ref, w1_ref, h1_ref, mask_ref, EDGES)
    carry(h1_ref, EDGES, 2)
    for n in (1, 2, 3, 4, 5, 6, 7, 8, 0):
        layer2(*chunks[n])
    carry(h2_ref, [(0, R2)], 4)
    for n in (3, 4, 5, 6, 7, 8, 0, 1, 2):
        layer3(*chunks[n])
        layer4(*chunks[n])
    p_ref[0, :, 0:TILE] = pltpu.roll(p_ref[0, :, TILES * TILE : (TILES + 1) * TILE], 1, 1)
    p_ref[2, :, (TILES + 1) * TILE : (TILES + 2) * TILE] = pltpu.roll(p_ref[2, :, TILE : 2 * TILE], TILE - 1, 1)
    tiles = [
        p_ref[0, :, k * TILE : (k + 1) * TILE]
        + p_ref[1, :, (k + 1) * TILE : (k + 2) * TILE]
        + p_ref[2, :, (k + 2) * TILE : (k + 3) * TILE]
        for k in range(TILES)
    ]
    col = iota((3 * TILE, 1), 0)
    tau = jnp.where(col < SEG, TILES * (col & 15) + (col >> 4), -1)
    order = onehot(tau == iota((1, TS), 1) + HALO)
    copies = []
    firsts, seconds = transposed(tiles[0:8]), transposed(tiles[8:16])
    for c in range(CL):
        third = pltpu.roll(tiles[16], TILE - 16 * c, 1) if c else tiles[16]
        noise = jnp.concatenate([firsts[c], seconds[c], third], axis=1)
        top = noise.astype(BF)
        rest = (noise - top.astype(F32)).astype(BF)
        both = dot(jnp.concatenate([top, rest], axis=0), order)
        out_ref[c] = stack_ref[c].astype(F32) - (both[0:MB] + both[MB:])
        copy = pltpu.make_async_copy(out_ref.at[c], out_hbm.at[c], sems.at[c])
        copy.start()
        copies.append(copy)
    for copy in copies:
        copy.wait()


def call(kernel, outs, scratch=(), smem=0, n=0, loose=0, name=None, limit=20, where=None):
    specs = [pl.BlockSpec(memory_space=pltpu.SMEM) for _ in range(smem)]
    specs += [pl.BlockSpec(memory_space=pltpu.VMEM) for _ in range(n)]
    specs += [pl.BlockSpec(memory_space=pl.ANY) for _ in range(loose)]
    number = len(outs) if isinstance(outs, tuple) else 1
    out_specs = tuple(pl.BlockSpec(memory_space=space) for space in where or (pltpu.VMEM,) * number)
    return pl.pallas_call(
        kernel,
        out_shape=outs,
        in_specs=specs,
        out_specs=out_specs if isinstance(outs, tuple) else out_specs[0],
        scratch_shapes=list(scratch),
        compiler_params=pltpu.CompilerParams(vmem_limit_bytes=limit * 2**20),
        name=name,
    )


def shape(*dims, dtype=BF):
    return pltpu.VMEM(dims, dtype)


def far(x):
    return pltpu.with_memory_space_constraint(x, pltpu.HBM)


def near(x):
    return pltpu.with_memory_space_constraint(x, pltpu.VMEM)


def build_send(dest, cell, traces):
    outs = (jax.ShapeDtypeStruct((OWNERS, PAY, TILE), BF), jax.ShapeDtypeStruct((8, 128), F32))
    scratch = [pltpu.VMEM((OWNERS, PAY, TILE), BF), pltpu.SemaphoreType.DMA((4,))]
    scratch += [pltpu.VMEM((1, COUNT), jnp.int32), pltpu.VMEM((1, COUNT), jnp.int32), pltpu.VMEM((COUNT, TS), BF)]
    scratch += [pltpu.SemaphoreType.DMA((3,))]
    return call(send_kernel, outs, scratch, loose=3, name="send", where=(pl.ANY, pltpu.VMEM))(
        far(dest), far(cell), far(traces)
    )


def build_weights(w_first, w_mid, w_last, bias, token):
    outs = (shape(R1 * CH, KDIM), shape(GROUP * CH, KDIM), shape(GROUP * CH, KDIM), shape(24, 160))
    return call(weights_kernel, outs, n=5, name="weights")(w_first, w_mid, w_last, bias, token)


def build_stack(recv, w1, pos):
    outs = (shape(CL, MB, TS), shape(MB, MB), shape(MB, MB))
    return call(stack_kernel, outs, n=1, loose=2, name="stack")(near(recv), w1, pos)


def reorder(stack, low, high):
    outs = (shape(MB, LANES), shape(HALO, LANES), shape(HALO, LANES))
    return call(swap_kernel, outs, n=3, name="reorder")(near(stack), near(low), near(high))


def inside(pos, core, w1):
    scratch = [pltpu.VMEM((80, 20 * TILE), BF), pltpu.VMEM((3, CH, WIDE), BF)]
    return call(inner_kernel, shape(R1 * CH, EXT), scratch, smem=1, n=2, name="inner")(pos, near(core), near(w1))


def convolve(pos, core, low, high, inner, stack, weights):
    scratch = [
        pltpu.VMEM((CL, MB, TS), F32),
        pltpu.SemaphoreType.DMA((CL,)),
        pltpu.VMEM((80, 20 * TILE), BF),
        pltpu.VMEM((80 * CH, EXT), BF),
        pltpu.VMEM((R2 * CH, EXT), BF),
        pltpu.VMEM((R3 * CH, WIDE), BF),
        pltpu.VMEM((3, MB, 20 * TILE), F32),
        pltpu.VMEM((3, CH, WIDE), BF),
    ]
    return call(conv_kernel, jax.ShapeDtypeStruct((CL, MB, TS), F32), scratch, smem=1, n=9, name="conv", limit=40, where=(pl.ANY,))(
        pos, near(core), near(low), near(high), near(inner), near(stack), *[near(w) for w in weights]
    )


def neighbours(low_edge, high_edge, axis):
    count = lax.axis_size(axis)
    up = [(i, i + 1) for i in range(count - 1)]
    down = [(b, a) for a, b in up]
    return lax.ppermute(high_edge, axis, up), lax.ppermute(low_edge, axis, down)


def shards(traces, dest, cell, w_first, w_mid, w_last, bias):
    send, token = build_send(dest.reshape(1, COUNT), cell.reshape(1, COUNT), traces)
    recv = lax.all_to_all(send, ("offset", "mid"), split_axis=0, concat_axis=0, tiled=True)
    weights = build_weights(w_first, w_mid, w_last, bias, token)
    pos = jnp.stack([lax.axis_index("mid"), lax.axis_index("tm")]).astype(jnp.int32)
    stack, left, right = build_stack(recv, weights[0], pos)
    low, high = neighbours(left, right, "tm")
    core, first, last = reorder(stack, low, high)
    below, above = neighbours(first, last, "mid")
    inner = inside(pos, core, weights[0])
    return convolve(pos, core, below, above, inner, stack, weights)


def solution(mesh):
    rows = P(("offset", "mid"), "tm")
    column = P(("offset", "mid"), None)
    placed = (rows, column, column, P(), P(), P(), P())
    return jax.shard_map(
        shards, mesh=mesh, in_specs=placed, out_specs=P("offset", "mid", "tm"), check_vma=False
    )
```
